128 devices in a mesh: tm: 16 (over z, x), gauge: 8 (over y, core).
Axes of the slice: x: 4, y: 4, z: 4, core: 2. Of those that a mesh axis runs over, the one named last changes fastest.
Arguments:
- records: bfloat16 [262144, 1536], P('tm', 'gauge'), may hold values from -400 to 400
- offsets: int32 [256], P('tm'), may hold values from 0 to 960
- column_map: int32 [1536], replicated, may hold values from 0 to 1535, each once
- angles: float32 [512], replicated, may hold values from -3.140625 to 3.140625
Outputs:
- factor: float32 [1536, 1536], replicated
The draws below stay inside these ranges and needn't reach their ends.
All inputs are finite; a program needn't handle non-finite values.
Results may differ from the reference program's by a relative error of at most 0.0014.
Values may be sent and summed in bfloat16 or wider, within the bound.
No kernel may reach another device: no remote copies, remote signals or barrier semaphores. Data moves between devices by JAX's collectives and lax.ppermute only.
A program may use at most 128 MiB of HBM per device.

```python
import math
import jax
import jax.numpy as jnp
from jax import lax

GAUGES = 512
COLS = 1536
BLOCK = 1024
BAND = 64
SAMPLES = 262144
NBLOCKS = 256


def draw_records(key, part):
    keys = jax.random.split(key, 4)
    nblocks = SAMPLES // BLOCK
    scales = jnp.exp(jax.random.uniform(keys[0], (COLS,), jnp.float32, 0.0, math.log(10.0)))
    noise = jnp.clip(jax.random.normal(keys[1], (SAMPLES, COLS), jnp.float32), -5.0, 5.0)
    level = 3.0 * jnp.clip(jax.random.normal(keys[2], (nblocks, 1, COLS), jnp.float32), -4.0, 4.0)
    slope = 4.0 * jnp.clip(jax.random.normal(keys[3], (nblocks, 1, COLS), jnp.float32), -4.0, 4.0)
    ramp = (jnp.arange(BLOCK, dtype=jnp.float32) / BLOCK - 0.5)[None, :, None]
    drift = (level + slope * ramp).reshape(SAMPLES, COLS)
    return (scales[None, :] * (noise + drift)).astype(jnp.bfloat16)


def touch_ends(values, own_key, smallest, largest):
    shape = values.shape
    index_at = [jax.random.randint(jax.random.fold_in(own_key, axis), (), 0, shape[axis]) for axis in range(len(shape))]
    values = values.at[tuple(index_at)].set(smallest)
    longest = shape.index(max(shape))
    index_at[longest] = (index_at[longest] + 1) % shape[longest]
    return values.at[tuple(index_at)].set(largest)


def setup_inputs(seed: int = 0) -> dict:
    arg_keys = jax.random.split(jax.random.key(seed), 5)
    return {
        "records": draw_records(jax.random.fold_in(arg_keys[4], 71), 0),
        "offsets": touch_ends(jax.random.randint(arg_keys[1], (NBLOCKS,), 0, BLOCK - BAND + 1), jax.random.fold_in(arg_keys[1], 1), 0, BLOCK - BAND).astype(jnp.int32),
        "column_map": jax.random.permutation(arg_keys[2], COLS).astype(jnp.int32),
        "angles": jnp.clip(jax.random.uniform(arg_keys[3], (GAUGES,), jnp.float32, -3.140625, 3.140625), -3.140625, 3.140625),
    }


def band_mask(offsets_here, total_rows):
    positions = jnp.arange(total_rows, dtype=jnp.int32)
    block_of = positions // BLOCK
    within = positions % BLOCK
    blocks = jnp.arange(offsets_here.shape[0], dtype=jnp.int32)
    inside = (block_of[None, :] == blocks[:, None]) & (within[None, :] >= offsets_here[:, None]) & (within[None, :] < offsets_here[:, None] + BAND)
    return inside.astype(jnp.bfloat16)

def drift_filter(rows, offsets_here):
    masks = band_mask(offsets_here, rows.shape[0])
    baseline = jnp.dot(masks.astype(jnp.float32), rows.astype(jnp.float32), preferred_element_type=jnp.float32) / BAND
    nblocks = offsets_here.shape[0]
    shaped = rows.astype(jnp.float32).reshape(nblocks, BLOCK, rows.shape[1]) - baseline[:, None, :]
    return shaped.reshape(rows.shape[0], rows.shape[1]).astype(jnp.bfloat16)

def rosette_rotate(full_rows, column_map, angles):
    count = angles.shape[0]
    picked = jnp.take(full_rows, column_map, axis=1)
    first_arm = picked[:, :count].astype(jnp.float32)
    middle_arm = picked[:, count:2 * count].astype(jnp.float32)
    last_arm = picked[:, 2 * count:].astype(jnp.float32)
    shear = 2.0 * middle_arm - first_arm - last_arm
    cosine = jnp.cos(angles)[None, :]
    sine = jnp.sin(angles)[None, :]
    cos_sq = cosine * cosine
    sin_sq = sine * sine
    mixed = sine * cosine
    along_x = first_arm * cos_sq + last_arm * sin_sq + shear * mixed
    along_y = first_arm * sin_sq + last_arm * cos_sq - shear * mixed
    shear_new = 2.0 * (last_arm - first_arm) * mixed + shear * (cos_sq - sin_sq)
    return jnp.concatenate([along_x, along_y, shear_new], axis=1).astype(jnp.bfloat16)

def gram_of(rotated):
    return lax.dot_general(rotated.astype(jnp.float32), rotated.astype(jnp.float32), (((0,), (0,)), ((), ())), preferred_element_type=jnp.float32)

def reference(records, offsets, column_map, angles):
    blocks = records.reshape(NBLOCKS, BLOCK, COLS)

    def accumulate(total, item):
        rows, offset_one = item
        filtered = drift_filter(rows, offset_one[None])
        rotated = rosette_rotate(filtered, column_map, angles)
        return (total + gram_of(rotated), None)
    total, unused = lax.scan(accumulate, jnp.zeros((COLS, COLS), jnp.float32), (blocks, offsets))
    return jnp.linalg.cholesky(total / SAMPLES).T
```

```python
import functools

import jax
import jax.numpy as jnp
from jax import lax
from jax.experimental import pallas as pl
from jax.experimental.pallas import tpu as pltpu
from jax.sharding import Mesh
from jax.sharding import PartitionSpec as P

BLOCK = 1024
BAND = 64
TILE = 128
CORES = 2
SAMPLE_AXES = ("z", "x")
GAUGE_AXES = ("y", "core")
PLANE_AXES = ("z", "x", "y")
HIGHEST = lax.Precision.HIGHEST
VMEM_BYTES = 56 * 1024 * 1024


def block_index(nb, i, j):
    return sum(nb - k for k in range(i)) + (j - i)


def half_blocks(nb):
    return -(-(nb * (nb + 1) // 2) // (4 * CORES)) * 4


def filter_kernel(chunk, nchunk, offsets, x_ref, out_ref):
    start = offsets[pl.program_id(0) * nchunk + chunk]
    x = x_ref[...].astype(jnp.float32)
    lane = lax.broadcasted_iota(jnp.int32, x.shape, 1)
    inside = (lane >= start) & (lane < start + BAND)
    baseline = jnp.sum(jnp.where(inside, x, 0.0), axis=1, keepdims=True) * (1.0 / BAND)
    out_ref[0] = (x - baseline).astype(out_ref.dtype)


def filter_chunk(records_t, offsets, chunk, nchunk, parts):
    rows = records_t.shape[0]
    return pl.pallas_call(
        functools.partial(filter_kernel, chunk, nchunk),
        out_shape=jax.ShapeDtypeStruct((parts, rows, BLOCK), jnp.bfloat16),
        grid_spec=pltpu.PrefetchScalarGridSpec(
            num_scalar_prefetch=1,
            grid=(parts,),
            in_specs=[pl.BlockSpec((rows, BLOCK), lambda d, off: (0, d * nchunk + chunk))],
            out_specs=pl.BlockSpec((1, rows, BLOCK), lambda d, off: (d, 0, 0)),
        ),
        compiler_params=pltpu.CompilerParams(vmem_limit_bytes=VMEM_BYTES),
        name="drift_filter",
    )(offsets, records_t)


def gram_kernel(first, core, *refs):
    if first:
        pick_ref, ft_ref, coef_ref, mine_out, other_out, rt_ref, acc_ref, sem = refs
        mine_in = other_in = None
    else:
        pick_ref, ft_ref, coef_ref, mine_in, other_in, mine_out, other_out, rt_ref, acc_ref, sem = refs
    step = pl.program_id(0)
    me = core[0]

    def loads():
        return (
            pltpu.make_async_copy(mine_in, acc_ref.at[me], sem.at[0]),
            pltpu.make_async_copy(other_in, acc_ref.at[1 - me], sem.at[1]),
        )

    if not first:

        @pl.when(step == 0)
        def _():
            for copy in loads():
                copy.start()

    ft = ft_ref[...]
    gauges = pick_ref.shape[1]
    samples = ft.shape[1]
    first_arm, middle_arm, last_arm = (
        jnp.dot(pick_ref[k], ft, preferred_element_type=jnp.float32) for k in range(3)
    )
    shear = 2.0 * middle_arm - first_arm - last_arm
    cos_sq, sin_sq, mixed = (
        jnp.broadcast_to(coef_ref[k][:, 0:1], (gauges, samples)) for k in range(3)
    )
    twist = shear * mixed
    along_x = first_arm * cos_sq + last_arm * sin_sq + twist
    along_y = first_arm * sin_sq + last_arm * cos_sq - twist
    shear_new = 2.0 * (last_arm - first_arm) * mixed + shear * (cos_sq - sin_sq)
    per_arm = rt_ref.shape[0] // 3
    here = pl.multiple_of(step * gauges, gauges)
    for k, value in enumerate((along_x, along_y, shear_new)):
        rt_ref[pl.ds(k * per_arm + here, gauges), :] = value.astype(jnp.bfloat16)

    @pl.when(step == pl.num_programs(0) - 1)
    def _():
        if not first:
            for copy in loads():
                copy.wait()
        nb = rt_ref.shape[0] // TILE
        used = nb * (nb + 1) // 2
        if first:
            for idx in range(used, CORES * acc_ref.shape[1]):
                acc_ref[idx % CORES, idx // CORES] = jnp.zeros((TILE, TILE), jnp.float32)
        for j in range(0, nb, 2):
            cols = rt_ref[TILE * j : TILE * (j + 2), :]
            rows = rt_ref[0 : TILE * (j + 2), :]
            part = lax.dot_general(
                rows, cols, (((1,), (1,)), ((), ())), preferred_element_type=jnp.float32
            )
            for i in range(j + 2):
                for jj in range(max(i, j), j + 2):
                    idx = block_index(nb, i, jj)
                    block = part[TILE * i : TILE * (i + 1), TILE * (jj - j) : TILE * (jj - j + 1)]
                    if first:
                        acc_ref[idx % CORES, idx // CORES] = block
                    else:
                        acc_ref[idx % CORES, idx // CORES] += block
        stores = (
            pltpu.make_async_copy(acc_ref.at[me], mine_out, sem.at[0]),
            pltpu.make_async_copy(acc_ref.at[1 - me], other_out, sem.at[1]),
        )
        for copy in stores:
            copy.start()
        for copy in stores:
            copy.wait()


def gram_chunk(core, pick, ft, coef, so_far):
    per_arm, cols = pick.shape[1], pick.shape[2]
    samples = ft.shape[1]
    half = half_blocks(cols // TILE)
    shape = jax.ShapeDtypeStruct((half, TILE, TILE), jnp.float32)
    anywhere = pl.BlockSpec(memory_space=pl.ANY)
    return pl.pallas_call(
        functools.partial(gram_kernel, so_far is None),
        out_shape=(shape, shape),
        grid_spec=pltpu.PrefetchScalarGridSpec(
            num_scalar_prefetch=1,
            grid=(per_arm // TILE,),
            in_specs=[
                pl.BlockSpec((3, TILE, cols), lambda g, core: (0, g, 0)),
                pl.BlockSpec((cols, samples), lambda g, core: (0, 0)),
                pl.BlockSpec((3, TILE, TILE), lambda g, core: (0, g, 0)),
            ]
            + ([] if so_far is None else [anywhere, anywhere]),
            out_specs=(anywhere, anywhere),
            scratch_shapes=[
                pltpu.VMEM((cols, samples), jnp.bfloat16),
                pltpu.VMEM((CORES, half, TILE, TILE), jnp.float32),
                pltpu.SemaphoreType.DMA((2,)),
            ],
        ),
        compiler_params=pltpu.CompilerParams(vmem_limit_bytes=VMEM_BYTES),
        name="rotate_gram",
    )(core, pick, ft, coef, *(() if so_far is None else so_far))


def dot_tn(a, b):
    return lax.dot_general(
        a, b, (((0,), (0,)), ((), ())), precision=HIGHEST, preferred_element_type=jnp.float32
    )


def dot_nn(a, b):
    return lax.dot_general(
        a, b, (((1,), (0,)), ((), ())), precision=HIGHEST, preferred_element_type=jnp.float32
    )


def factor_block(a_ref, e_ref):
    lane = lax.broadcasted_iota(jnp.int32, (8, TILE), 1)
    sub = lax.broadcasted_iota(jnp.int32, (8, TILE), 0)
    rows = lax.broadcasted_iota(jnp.int32, (TILE, TILE), 0)
    cols = lax.broadcasted_iota(jnp.int32, (TILE, TILE), 1)
    e_ref[...] = (rows == cols).astype(jnp.float32)

    def strip(s, carry):
        r0 = pl.multiple_of(8 * s, 8)
        cur = a_ref[pl.ds(r0, 8), :]
        ecur = e_ref[pl.ds(r0, 8), :]
        d = [
            jnp.take_along_axis(cur, jnp.full((8, TILE), r0 + j, jnp.int32), axis=1)
            for j in range(8)
        ]
        for j in range(7):
            m = jnp.where(sub > j, d[j] * (1.0 / d[j][j : j + 1, :]), 0.0)
            cur = cur - m * cur[j : j + 1, :]
            ecur = ecur - m * ecur[j : j + 1, :]
            for k in range(j + 1, 8):
                d[k] = d[k] - m * d[k][j : j + 1, :]
        pivot = d[0]
        for j in range(1, 8):
            pivot = jnp.where(sub == j, d[j], pivot)
        scale = lax.rsqrt(pivot)
        cur = jnp.where(lane >= r0 + sub, cur * scale, 0.0)
        ecur = ecur * scale
        later = jnp.where(lane >= r0 + 8, cur, 0.0)
        a_ref[...] -= dot_tn(later, cur)
        e_ref[...] -= dot_tn(later, ecur)
        a_ref[pl.ds(r0, 8), :] = cur
        e_ref[pl.ds(r0, 8), :] = ecur
        return carry

    lax.fori_loop(0, TILE // 8, strip, 0)


def cholesky_kernel(scale, core, mine_ref, other_ref, u_ref, g_ref, a_ref, e_ref, s_ref, sem):
    me = core[0]
    loads = (
        pltpu.make_async_copy(mine_ref, g_ref.at[me], sem.at[0]),
        pltpu.make_async_copy(other_ref, g_ref.at[1 - me], sem.at[1]),
    )
    for copy in loads:
        copy.start()
    for copy in loads:
        copy.wait()
    size = u_ref.shape[0]
    nb = size // TILE
    for r0 in range(0, size, 2 * TILE):
        u_ref[r0 : r0 + 2 * TILE, :] = jnp.zeros((2 * TILE, size), jnp.float32)
        for h in range(2):
            i = r0 // TILE + h
            for j in range(i, nb):
                idx = block_index(nb, i, j)
                s_ref[TILE * h : TILE * (h + 1), TILE * j : TILE * (j + 1)] = (
                    g_ref[idx % CORES, idx // CORES] * scale
                )
        for h in range(2):
            c0 = r0 + TILE * h
            here = slice(TILE * h, TILE * (h + 1))
            if r0:
                s_ref[here, c0:] -= dot_tn(u_ref[0:r0, c0 : c0 + TILE], u_ref[0:r0, c0:])
        for h in range(2):
            c0 = r0 + TILE * h
            here = slice(TILE * h, TILE * (h + 1))
            if h:
                s_ref[here, c0:] -= dot_tn(u_ref[r0:c0, c0 : c0 + TILE], u_ref[r0:c0, c0:])
            a_ref[...] = s_ref[here, c0 : c0 + TILE]
            factor_block(a_ref, e_ref)
            u_ref[c0 : c0 + TILE, c0 : c0 + TILE] = a_ref[...]
            if c0 + TILE < size:
                u_ref[c0 : c0 + TILE, c0 + TILE :] = dot_nn(e_ref[...], s_ref[here, c0 + TILE :])


def cholesky_blocks(core, mine, other, size, scale):
    half = mine.shape[0]
    anywhere = pl.BlockSpec(memory_space=pl.ANY)
    return pl.pallas_call(
        functools.partial(cholesky_kernel, scale),
        out_shape=jax.ShapeDtypeStruct((size, size), jnp.float32),
        grid_spec=pltpu.PrefetchScalarGridSpec(
            num_scalar_prefetch=1,
            grid=(1,),
            in_specs=[anywhere, anywhere],
            out_specs=pl.BlockSpec((size, size), lambda g, core: (0, 0), pipeline_mode=pl.Buffered(1)),
            scratch_shapes=[
                pltpu.VMEM((CORES, half, TILE, TILE), jnp.float32),
                pltpu.VMEM((TILE, TILE), jnp.float32),
                pltpu.VMEM((TILE, TILE), jnp.float32),
                pltpu.VMEM((2 * TILE, size), jnp.float32),
                pltpu.SemaphoreType.DMA((2,)),
            ],
        ),
        compiler_params=pltpu.CompilerParams(vmem_limit_bytes=VMEM_BYTES),
        name="cholesky",
    )(core, mine, other)


def swap_cores(x):
    return lax.ppermute(x, "core", [(0, 1), (1, 0)])


def gather_plane(x):
    plane = lax.axis_size(PLANE_AXES)
    copies = jnp.broadcast_to(x[None], (plane, *x.shape))
    return lax.all_to_all(copies, PLANE_AXES, split_axis=0, concat_axis=0, tiled=True)


def shards(records, offsets, column_map, angles):
    parts = lax.axis_size(GAUGE_AXES)
    rows, cols_here = records.shape
    cols = column_map.shape[0]
    per_arm = cols // 3
    nchunk = rows // BLOCK // parts
    core = lax.axis_index("core").astype(jnp.int32).reshape(1)
    records_t = records.T
    arms = column_map.reshape(3, per_arm, 1)
    pick = (arms == jnp.arange(cols, dtype=jnp.int32)[None, None, :]).astype(jnp.bfloat16)
    cosine, sine = jnp.cos(angles), jnp.sin(angles)
    coef = jnp.stack([cosine * cosine, sine * sine, sine * cosine])
    coef = jnp.broadcast_to(coef[:, :, None], (3, per_arm, TILE))
    chunks = [filter_chunk(records_t, offsets, c, nchunk, parts) for c in range(nchunk)]
    acc = None
    for filtered in chunks:
        regrouped = lax.all_to_all(filtered, GAUGE_AXES, split_axis=0, concat_axis=0, tiled=True)
        acc = gram_chunk(core, pick, regrouped.reshape(cols, BLOCK), coef, acc)
    mine, other = acc
    half = mine.shape[0]
    mine = mine + swap_cores(other)
    plane = lax.axis_size(PLANE_AXES)
    share = half * TILE // plane
    spread = lax.all_to_all(
        mine.reshape(plane, share, TILE), PLANE_AXES, split_axis=0, concat_axis=0, tiled=True
    )
    mine = gather_plane(spread.sum(0)).reshape(half, TILE, TILE)
    other = swap_cores(mine)
    total = rows * lax.axis_size(SAMPLE_AXES)
    return cholesky_blocks(core, mine, other, cols, 1.0 / total)


def solution(mesh):
    devices = mesh.devices
    tm, gauge = devices.shape
    side = int(round(tm**0.5))
    fine = Mesh(
        devices.reshape(side, tm // side, gauge // CORES, CORES), SAMPLE_AXES + GAUGE_AXES
    )
    placed = (P(SAMPLE_AXES, GAUGE_AXES), P(SAMPLE_AXES), P(), P())
    return jax.shard_map(shards, mesh=fine, in_specs=placed, out_specs=P(), check_vma=False)
```

```python
import functools

import jax
import jax.numpy as jnp
from jax import lax
from jax.experimental import pallas as pl
from jax.experimental.pallas import tpu as pltpu
from jax.sharding import Mesh
from jax.sharding import PartitionSpec as P

BLOCK = 1024
BAND = 64
TILE = 128
CORES = 2
SAMPLE_AXES = ("z", "x")
GAUGE_AXES = ("y", "core")
PLANE_AXES = ("z", "x", "y")
HIGHEST = lax.Precision.HIGHEST
VMEM_BYTES = 56 * 1024 * 1024


def block_index(nb, i, j):
    return sum(nb - k for k in range(i)) + (j - i)


def half_blocks(nb):
    return -(-(nb * (nb + 1) // 2) // (4 * CORES)) * 4


def filter_kernel(blocks, offsets, x_ref, head_ref, tail_ref):
    split = head_ref.shape[2]
    for b in range(blocks):
        start = offsets[pl.program_id(0) * blocks + b]
        x = x_ref[:, b * BLOCK : (b + 1) * BLOCK]
        sample = lax.broadcasted_iota(jnp.int32, (BLOCK, TILE), 0)
        inside = jnp.where((sample >= start) & (sample < start + BAND), 1.0, 0.0)
        total = jnp.dot(x, inside.astype(jnp.bfloat16), preferred_element_type=jnp.float32)
        baseline = total * (1.0 / BAND)
        for t in range(0, BLOCK, TILE):
            value = (x[:, t : t + TILE].astype(jnp.float32) - baseline).astype(jnp.bfloat16)
            here = b * BLOCK + t
            if here < split:
                head_ref[0, :, here : here + TILE] = value
            else:
                tail_ref[0, :, here - split : here - split + TILE] = value


def filter_records(records_t, offsets, parts):
    rows, samples = records_t.shape
    each = samples // parts
    tail = BLOCK // 2
    widths = (each - tail, tail)
    return pl.pallas_call(
        functools.partial(filter_kernel, each // BLOCK),
        out_shape=tuple(jax.ShapeDtypeStruct((parts, rows, w), jnp.bfloat16) for w in widths),
        grid_spec=pltpu.PrefetchScalarGridSpec(
            num_scalar_prefetch=1,
            grid=(parts,),
            in_specs=[pl.BlockSpec((rows, each), lambda d, off: (0, d))],
            out_specs=tuple(pl.BlockSpec((1, rows, w), lambda d, off: (d, 0, 0)) for w in widths),
        ),
        compiler_params=pltpu.CompilerParams(vmem_limit_bytes=VMEM_BYTES),
        name="drift_filter",
    )(offsets, records_t)


def gram_kernel(first, core, *refs):
    if first:
        pick_ref, ft_ref, coef_ref, mine_out, other_out, rt_ref, acc_ref, sem = refs
        mine_in = other_in = None
    else:
        pick_ref, ft_ref, coef_ref, mine_in, other_in, mine_out, other_out, rt_ref, acc_ref, sem = refs
    step = pl.program_id(0)
    me = core[0]

    def loads():
        return (
            pltpu.make_async_copy(mine_in, acc_ref.at[me], sem.at[0]),
            pltpu.make_async_copy(other_in, acc_ref.at[1 - me], sem.at[1]),
        )

    if not first:

        @pl.when(step == 0)
        def _():
            for copy in loads():
                copy.start()

    ft = ft_ref[...]
    gauges = pick_ref.shape[1]
    samples = ft.shape[1]
    first_arm, middle_arm, last_arm = (
        jnp.dot(pick_ref[k], ft, preferred_element_type=jnp.float32) for k in range(3)
    )
    shear = 2.0 * middle_arm - first_arm - last_arm
    cos_sq, sin_sq, mixed = (
        jnp.broadcast_to(coef_ref[k][:, 0:1], (gauges, samples)) for k in range(3)
    )
    twist = shear * mixed
    along_x = first_arm * cos_sq + last_arm * sin_sq + twist
    along_y = first_arm * sin_sq + last_arm * cos_sq - twist
    shear_new = 2.0 * (last_arm - first_arm) * mixed + shear * (cos_sq - sin_sq)
    per_arm = rt_ref.shape[0] // 3
    here = pl.multiple_of(step * gauges, gauges)
    for k, value in enumerate((along_x, along_y, shear_new)):
        rt_ref[pl.ds(k * per_arm + here, gauges), :] = value.astype(jnp.bfloat16)

    @pl.when(step == pl.num_programs(0) - 1)
    def _():
        if not first:
            for copy in loads():
                copy.wait()
        nb = rt_ref.shape[0] // TILE
        used = nb * (nb + 1) // 2
        if first:
            for idx in range(used, CORES * acc_ref.shape[1]):
                acc_ref[idx % CORES, idx // CORES] = jnp.zeros((TILE, TILE), jnp.float32)
        for j in range(0, nb, 2):
            cols = rt_ref[TILE * j : TILE * (j + 2), :]
            rows = rt_ref[0 : TILE * (j + 2), :]
            part = lax.dot_general(
                rows, cols, (((1,), (1,)), ((), ())), preferred_element_type=jnp.float32
            )
            for i in range(j + 2):
                for jj in range(max(i, j), j + 2):
                    idx = block_index(nb, i, jj)
                    block = part[TILE * i : TILE * (i + 1), TILE * (jj - j) : TILE * (jj - j + 1)]
                    if first:
                        acc_ref[idx % CORES, idx // CORES] = block
                    else:
                        acc_ref[idx % CORES, idx // CORES] += block
        stores = (
            pltpu.make_async_copy(acc_ref.at[me], mine_out, sem.at[0]),
            pltpu.make_async_copy(acc_ref.at[1 - me], other_out, sem.at[1]),
        )
        for copy in stores:
            copy.start()
        for copy in stores:
            copy.wait()


def gram_chunk(core, pick, ft, coef, so_far):
    per_arm, cols = pick.shape[1], pick.shape[2]
    samples = ft.shape[1]
    half = half_blocks(cols // TILE)
    shape = jax.ShapeDtypeStruct((half, TILE, TILE), jnp.float32)
    anywhere = pl.BlockSpec(memory_space=pl.ANY)
    return pl.pallas_call(
        functools.partial(gram_kernel, so_far is None),
        out_shape=(shape, shape),
        grid_spec=pltpu.PrefetchScalarGridSpec(
            num_scalar_prefetch=1,
            grid=(per_arm // TILE,),
            in_specs=[
                pl.BlockSpec((3, TILE, cols), lambda g, core: (0, g, 0)),
                pl.BlockSpec((cols, samples), lambda g, core: (0, 0)),
                pl.BlockSpec((3, TILE, TILE), lambda g, core: (0, g, 0)),
            ]
            + ([] if so_far is None else [anywhere, anywhere]),
            out_specs=(anywhere, anywhere),
            scratch_shapes=[
                pltpu.VMEM((cols, samples), jnp.bfloat16),
                pltpu.VMEM((CORES, half, TILE, TILE), jnp.float32),
                pltpu.SemaphoreType.DMA((2,)),
            ],
        ),
        compiler_params=pltpu.CompilerParams(vmem_limit_bytes=VMEM_BYTES),
        name="rotate_gram",
    )(core, pick, ft, coef, *(() if so_far is None else so_far))


def dot_tn(a, b):
    return lax.dot_general(
        a, b, (((0,), (0,)), ((), ())), precision=HIGHEST, preferred_element_type=jnp.float32
    )


def dot_nn(a, b):
    return lax.dot_general(
        a, b, (((1,), (0,)), ((), ())), precision=HIGHEST, preferred_element_type=jnp.float32
    )


def split3(x):
    high = x.astype(jnp.bfloat16).astype(jnp.float32)
    rest = x - high
    middle = rest.astype(jnp.bfloat16).astype(jnp.float32)
    return high, middle, rest - middle


def outer_product(a, b):
    a1, a2, a3 = split3(a)
    b1, b2, b3 = split3(b)
    left = jnp.concatenate([a1, a1, a2, a2, a1, a3], axis=0).astype(jnp.bfloat16)
    right = jnp.concatenate([b1, b2, b1, b2, b3, b1], axis=0).astype(jnp.bfloat16)
    return lax.dot_general(
        left, right, (((0,), (0,)), ((), ())), preferred_element_type=jnp.float32
    )


def factor_block(a_ref, e_ref):
    lane = lax.broadcasted_iota(jnp.int32, (8, TILE), 1)
    sub = lax.broadcasted_iota(jnp.int32, (8, TILE), 0)
    strips = TILE // 8
    work = [a_ref[8 * t : 8 * t + 8, :] for t in range(strips)]

    def columns(x, r0):
        return [jnp.broadcast_to(x[:, r0 + j : r0 + j + 1], (8, TILE)) for j in range(8)]

    def row_of(x, j):
        return jnp.broadcast_to(x[j : j + 1, :], (8, TILE))

    for s in range(strips):
        r0 = 8 * s
        last = s == strips - 1
        here = (lane >= r0) & (lane < r0 + 8)
        top = columns(work[s], r0)
        cur = jnp.where(here, jnp.where(lane == r0 + sub, 1.0, 0.0), work[s])
        if not last:
            low = columns(work[s + 1], r0)
            nxt = jnp.where(here, 0.0, work[s + 1])
        for j in range(8):
            inv = 1.0 / row_of(top[j], j)
            m_top = jnp.where(sub > j, top[j] * inv, 0.0)
            m_low = None if last else low[j] * inv
            for k in range(j + 1, 8):
                c = row_of(top[k], j)
                if k == j + 1:
                    top[k] = top[k] - jnp.where(sub > j, top[j] * c, 0.0) * inv
                else:
                    top[k] = top[k] - m_top * c
                if not last:
                    low[k] = low[k] - m_low * c
            row = row_of(cur, j)
            cur = cur - m_top * row
            if not last:
                nxt = nxt - m_low * row
        pivot = top[0]
        for j in range(1, 8):
            pivot = jnp.where(sub == j, top[j], pivot)
        scale = lax.rsqrt(pivot)
        cur = cur * scale
        later = jnp.where(lane >= r0 + 8, cur, 0.0)
        out = later
        for k in range(8):
            out = jnp.where((lane == r0 + k) & (sub <= k), top[k] * scale, out)
        a_ref[r0 : r0 + 8, :] = out
        e_ref[r0 : r0 + 8, :] = jnp.where(lane < r0 + 8, cur, 0.0)
        if not last:
            work[s + 1] = nxt
        if s + 2 < strips:
            update = outer_product(later, cur)
            for t in range(s + 2, strips):
                work[t] = jnp.where(here, 0.0, work[t]) - update[8 * t : 8 * t + 8, :]


def cholesky_kernel(
    scale, core, mine_ref, other_ref, out_ref, u_ref, g_ref, a_ref, e_ref, s_ref, in_sem, out_sem
):
    me = core[0]
    size = u_ref.shape[0]
    nb = size // TILE
    early = nb
    pieces = ((0, early), (early, g_ref.shape[1]))

    def loads(k):
        lo, hi = pieces[k]
        return (
            pltpu.make_async_copy(mine_ref.at[lo:hi], g_ref.at[me, lo:hi], in_sem.at[2 * k]),
            pltpu.make_async_copy(
                other_ref.at[lo:hi], g_ref.at[1 - me, lo:hi], in_sem.at[2 * k + 1]
            ),
        )

    def store(k):
        rows = slice(TILE * k, TILE * (k + 1))
        return pltpu.make_async_copy(u_ref.at[rows], out_ref.at[rows], out_sem.at[k])

    for k in range(2):
        for copy in loads(k):
            copy.start()

    def body(i, carry):
        for k in range(nb):
            h = k % 2
            r0 = TILE * (k - h)
            c0 = TILE * k

            @pl.when(i == k)
            def _(k=k, h=h, r0=r0, c0=c0):
                if k == 0 or k == 2:
                    for copy in loads(k // 2):
                        copy.wait()
                if h == 0:
                    for hh in range(2):
                        for j in range(k + hh, nb):
                            idx = block_index(nb, k + hh, j)
                            s_ref[TILE * hh : TILE * (hh + 1), TILE * j : TILE * (j + 1)] = (
                                g_ref[idx % CORES, idx // CORES] * scale
                            )
                        if r0:
                            first = c0 + TILE * hh
                            s_ref[TILE * hh : TILE * (hh + 1), first:] -= dot_tn(
                                u_ref[0:r0, first : first + TILE], u_ref[0:r0, first:]
                            )
                else:
                    s_ref[TILE:, c0:] -= dot_tn(u_ref[r0:c0, c0 : c0 + TILE], u_ref[r0:c0, c0:])
                a_ref[...] = s_ref[TILE * h : TILE * (h + 1), c0 : c0 + TILE]

        factor_block(a_ref, e_ref)
        for k in range(nb):
            h = k % 2
            c0 = TILE * k

            @pl.when(i == k)
            def _(k=k, h=h, c0=c0):
                rows = slice(c0, c0 + TILE)
                if c0:
                    u_ref[rows, 0:c0] = jnp.zeros((TILE, c0), jnp.float32)
                u_ref[rows, c0 : c0 + TILE] = a_ref[...]
                if c0 + TILE < size:
                    u_ref[rows, c0 + TILE :] = dot_nn(
                        e_ref[...], s_ref[TILE * h : TILE * (h + 1), c0 + TILE :]
                    )
                store(k).start()

        return carry

    lax.fori_loop(0, nb, body, 0)
    for k in range(nb):
        store(k).wait()


def cholesky_blocks(core, mine, other, size, scale):
    half = mine.shape[0]
    anywhere = pl.BlockSpec(memory_space=pl.ANY)
    return pl.pallas_call(
        functools.partial(cholesky_kernel, scale),
        out_shape=jax.ShapeDtypeStruct((size, size), jnp.float32),
        grid_spec=pltpu.PrefetchScalarGridSpec(
            num_scalar_prefetch=1,
            grid=(1,),
            in_specs=[anywhere, anywhere],
            out_specs=anywhere,
            scratch_shapes=[
                pltpu.VMEM((size, size), jnp.float32),
                pltpu.VMEM((CORES, half, TILE, TILE), jnp.float32),
                pltpu.VMEM((TILE, TILE), jnp.float32),
                pltpu.VMEM((TILE, TILE), jnp.float32),
                pltpu.VMEM((2 * TILE, size), jnp.float32),
                pltpu.SemaphoreType.DMA((4,)),
                pltpu.SemaphoreType.DMA((size // TILE,)),
            ],
        ),
        compiler_params=pltpu.CompilerParams(vmem_limit_bytes=VMEM_BYTES),
        name="cholesky",
    )(core, mine, other)


def swap_cores(x):
    return lax.ppermute(x, "core", [(0, 1), (1, 0)])


def gather_plane(x):
    plane = lax.axis_size(PLANE_AXES)
    copies = jnp.broadcast_to(x[None], (plane, *x.shape))
    return lax.all_to_all(copies, PLANE_AXES, split_axis=0, concat_axis=0, tiled=True)


def shards(records, offsets, column_map, angles):
    parts = lax.axis_size(GAUGE_AXES)
    rows, cols_here = records.shape
    cols = column_map.shape[0]
    per_arm = cols // 3
    core = lax.axis_index("core").astype(jnp.int32).reshape(1)
    records_t = records.T
    arms = column_map.reshape(3, per_arm, 1)
    pick = (arms == jnp.arange(cols, dtype=jnp.int32)[None, None, :]).astype(jnp.bfloat16)
    cosine, sine = jnp.cos(angles), jnp.sin(angles)
    coef = jnp.stack([cosine * cosine, sine * sine, sine * cosine])
    coef = jnp.broadcast_to(coef[:, :, None], (3, per_arm, TILE))
    acc = None
    for filtered in filter_records(records_t, offsets, parts):
        regrouped = lax.all_to_all(filtered, GAUGE_AXES, split_axis=0, concat_axis=0, tiled=True)
        acc = gram_chunk(core, pick, regrouped.reshape(cols, -1), coef, acc)
    mine, other = acc
    half = mine.shape[0]
    mine = mine + swap_cores(other)
    plane = lax.axis_size(PLANE_AXES)
    share = half * TILE // plane
    spread = lax.all_to_all(
        mine.reshape(plane, share, TILE), PLANE_AXES, split_axis=0, concat_axis=0, tiled=True
    )
    mine = gather_plane(spread.sum(0)).reshape(half, TILE, TILE)
    other = swap_cores(mine)
    total = rows * lax.axis_size(SAMPLE_AXES)
    return cholesky_blocks(core, mine, other, cols, 1.0 / total)


def solution(mesh):
    devices = mesh.devices
    tm, gauge = devices.shape
    side = int(round(tm**0.5))
    fine = Mesh(
        devices.reshape(side, tm // side, gauge // CORES, CORES), SAMPLE_AXES + GAUGE_AXES
    )
    placed = (P(SAMPLE_AXES, GAUGE_AXES), P(SAMPLE_AXES), P(), P())
    return jax.shard_map(shards, mesh=fine, in_specs=placed, out_specs=P(), check_vma=False)
```

```python
import functools

import jax
import jax.numpy as jnp
from jax import lax
from jax.experimental import pallas as pl
from jax.experimental.pallas import tpu as pltpu
from jax.sharding import Mesh
from jax.sharding import PartitionSpec as P

BLOCK = 1024
BAND = 64
TILE = 128
CORES = 2
SAMPLE_AXES = ("z", "x")
GAUGE_AXES = ("y", "core")
PLANE_AXES = ("z", "x", "y")
HIGHEST = lax.Precision.HIGHEST
VMEM_BYTES = 56 * 1024 * 1024


def block_index(nb, i, j):
    return sum(nb - k for k in range(i)) + (j - i)


def half_blocks(nb):
    return -(-(nb * (nb + 1) // 2) // (4 * CORES)) * 4


def dot_nt(a, b):
    return lax.dot_general(a, b, (((1,), (1,)), ((), ())), preferred_element_type=jnp.float32)


def filter_kernel(blocks, offsets, x_ref, head_ref, tail_ref):
    split = head_ref.shape[2]
    for b in range(blocks):
        start = offsets[pl.program_id(0) * blocks + b]
        x = x_ref[:, b * BLOCK : (b + 1) * BLOCK]
        sample = lax.broadcasted_iota(jnp.int32, (1, BLOCK), 1)
        inside = jnp.where((sample >= start) & (sample < start + BAND), 1.0, 0.0)
        mask = jnp.broadcast_to(inside.astype(jnp.bfloat16), (TILE, BLOCK))
        total = dot_nt(x, mask)
        baseline = total * (1.0 / BAND)
        for t in range(0, BLOCK, TILE):
            value = (x[:, t : t + TILE].astype(jnp.float32) - baseline).astype(jnp.bfloat16)
            here = b * BLOCK + t
            if here < split:
                head_ref[0, :, here : here + TILE] = value
            else:
                tail_ref[0, :, here - split : here - split + TILE] = value


def filter_records(records_t, offsets, parts):
    rows, samples = records_t.shape
    each = samples // parts
    tail = BLOCK // 2
    widths = (each - tail, tail)
    return pl.pallas_call(
        functools.partial(filter_kernel, each // BLOCK),
        out_shape=tuple(jax.ShapeDtypeStruct((parts, rows, w), jnp.bfloat16) for w in widths),
        grid_spec=pltpu.PrefetchScalarGridSpec(
            num_scalar_prefetch=1,
            grid=(parts,),
            in_specs=[pl.BlockSpec((rows, each), lambda d, off: (0, d))],
            out_specs=tuple(pl.BlockSpec((1, rows, w), lambda d, off: (d, 0, 0)) for w in widths),
        ),
        compiler_params=pltpu.CompilerParams(vmem_limit_bytes=VMEM_BYTES),
        name="drift_filter",
    )(offsets, records_t)


def gram_kernel(first, core, *refs):
    if first:
        map_ref, ft_ref, angle_ref, mine_out, other_out, rt_ref, acc_ref, sem = refs
        mine_in = other_in = None
    else:
        map_ref, ft_ref, angle_ref, mine_in, other_in, mine_out, other_out, rt_ref, acc_ref, sem = refs
    step = pl.program_id(0)
    me = core[0]

    def loads():
        return (
            pltpu.make_async_copy(mine_in, acc_ref.at[me], sem.at[0]),
            pltpu.make_async_copy(other_in, acc_ref.at[1 - me], sem.at[1]),
        )

    if not first:

        @pl.when(step == 0)
        def _():
            for copy in loads():
                copy.start()

    ft = ft_ref[...]
    cols, samples = ft.shape
    lanes = map_ref.shape[1]
    steps = pl.num_programs(0)

    def down(row):
        return jnp.broadcast_to(row, (lanes, lanes)).T

    def arm(k):
        source = down(map_ref[pl.ds(k * steps + step, 1), :].astype(jnp.float32))
        index = lax.broadcasted_iota(jnp.int32, (lanes, lanes), 1).astype(jnp.float32)
        pick = [jnp.where(source - c == index, 1.0, 0.0) for c in range(0, cols, lanes)]
        pick = jnp.concatenate(pick, axis=1).astype(jnp.bfloat16)
        return jnp.dot(pick, ft, preferred_element_type=jnp.float32)

    first_arm, middle_arm, last_arm = (arm(k) for k in range(3))
    shear = 2.0 * middle_arm - first_arm - last_arm
    angle = angle_ref[pl.ds(step, 1), :]
    cosine, sine = jnp.cos(angle), jnp.sin(angle)
    cos_sq, sin_sq, mixed = (
        jnp.tile(down(c), (1, samples // lanes))
        for c in (cosine * cosine, sine * sine, sine * cosine)
    )
    twist = shear * mixed
    along_x = first_arm * cos_sq + last_arm * sin_sq + twist
    along_y = first_arm * sin_sq + last_arm * cos_sq - twist
    shear_new = 2.0 * (last_arm - first_arm) * mixed + shear * (cos_sq - sin_sq)
    per_arm = rt_ref.shape[0] // 3
    here = pl.multiple_of(step * lanes, lanes)
    for k, value in enumerate((along_x, along_y, shear_new)):
        rt_ref[pl.ds(k * per_arm + here, lanes), :] = value.astype(jnp.bfloat16)

    @pl.when(step == pl.num_programs(0) - 1)
    def _():
        if not first:
            for copy in loads():
                copy.wait()
        nb = rt_ref.shape[0] // TILE
        used = nb * (nb + 1) // 2
        if first:
            for idx in range(used, CORES * acc_ref.shape[1]):
                acc_ref[idx % CORES, idx // CORES] = jnp.zeros((TILE, TILE), jnp.float32)
        for j in range(0, nb, 2):
            cols = rt_ref[TILE * j : TILE * (j + 2), :]
            rows = rt_ref[0 : TILE * (j + 2), :]
            part = dot_nt(rows, cols)
            for i in range(j + 2):
                for jj in range(max(i, j), j + 2):
                    idx = block_index(nb, i, jj)
                    block = part[TILE * i : TILE * (i + 1), TILE * (jj - j) : TILE * (jj - j + 1)]
                    if first:
                        acc_ref[idx % CORES, idx // CORES] = block
                    else:
                        acc_ref[idx % CORES, idx // CORES] += block
        stores = (
            pltpu.make_async_copy(acc_ref.at[me], mine_out, sem.at[0]),
            pltpu.make_async_copy(acc_ref.at[1 - me], other_out, sem.at[1]),
        )
        for copy in stores:
            copy.start()
        for copy in stores:
            copy.wait()


def gram_chunk(core, arms, ft, angles, so_far):
    cols, samples = ft.shape
    half = half_blocks(cols // TILE)
    shape = jax.ShapeDtypeStruct((half, TILE, TILE), jnp.float32)
    anywhere = pl.BlockSpec(memory_space=pl.ANY)
    return pl.pallas_call(
        functools.partial(gram_kernel, so_far is None),
        out_shape=(shape, shape),
        grid_spec=pltpu.PrefetchScalarGridSpec(
            num_scalar_prefetch=1,
            grid=(angles.shape[0],),
            in_specs=[
                pl.BlockSpec(arms.shape, lambda g, core: (0, 0)),
                pl.BlockSpec((cols, samples), lambda g, core: (0, 0)),
                pl.BlockSpec(angles.shape, lambda g, core: (0, 0)),
            ]
            + ([] if so_far is None else [anywhere, anywhere]),
            out_specs=(anywhere, anywhere),
            scratch_shapes=[
                pltpu.VMEM((cols, samples), jnp.bfloat16),
                pltpu.VMEM((CORES, half, TILE, TILE), jnp.float32),
                pltpu.SemaphoreType.DMA((2,)),
            ],
        ),
        compiler_params=pltpu.CompilerParams(vmem_limit_bytes=VMEM_BYTES),
        name="rotate_gram",
    )(core, arms, ft, angles, *(() if so_far is None else so_far))


def dot_tn(a, b):
    return lax.dot_general(
        a, b, (((0,), (0,)), ((), ())), precision=HIGHEST, preferred_element_type=jnp.float32
    )


def dot_nn(a, b):
    return lax.dot_general(
        a, b, (((1,), (0,)), ((), ())), precision=HIGHEST, preferred_element_type=jnp.float32
    )


def split3(x):
    high = x.astype(jnp.bfloat16).astype(jnp.float32)
    rest = x - high
    middle = rest.astype(jnp.bfloat16).astype(jnp.float32)
    return high, middle, rest - middle


def outer_product(a, b):
    a1, a2, a3 = split3(a)
    b1, b2, b3 = split3(b)
    left = jnp.concatenate([a1, a1, a2, a2, a1, a3], axis=0).astype(jnp.bfloat16)
    right = jnp.concatenate([b1, b2, b1, b2, b3, b1], axis=0).astype(jnp.bfloat16)
    return lax.dot_general(
        left, right, (((0,), (0,)), ((), ())), preferred_element_type=jnp.float32
    )


def factor_block(a_ref, e_ref):
    lane = lax.broadcasted_iota(jnp.int32, (8, TILE), 1)
    sub = lax.broadcasted_iota(jnp.int32, (8, TILE), 0)
    strips = TILE // 8
    work = [a_ref[8 * t : 8 * t + 8, :] for t in range(strips)]

    def columns(x, r0):
        return [jnp.broadcast_to(x[:, r0 + j : r0 + j + 1], (8, TILE)) for j in range(8)]

    def row_of(x, j):
        return jnp.broadcast_to(x[j : j + 1, :], (8, TILE))

    top = columns(work[0], 0)
    for s in range(strips):
        r0 = 8 * s
        last = s == strips - 1
        here = (lane >= r0) & (lane < r0 + 8)
        cur = jnp.where(here, jnp.where(lane == r0 + sub, 1.0, 0.0), work[s])
        if not last:
            low = columns(work[s + 1], r0)
            top2 = columns(work[s], r0 + 8)
            low2 = columns(work[s + 1], r0 + 8)
            nxt = jnp.where(here, 0.0, work[s + 1])
        for j in range(8):
            inv = 1.0 / row_of(top[j], j)
            m_top = jnp.where(sub > j, top[j] * inv, 0.0)
            m_low = None if last else low[j] * inv
            for k in range(j + 1, 8):
                c = row_of(top[k], j)
                if k == j + 1:
                    top[k] = top[k] - jnp.where(sub > j, top[j] * c, 0.0) * inv
                else:
                    top[k] = top[k] - m_top * c
                if not last:
                    low[k] = low[k] - m_low * c
            if not last:
                for k in range(8):
                    c = row_of(top2[k], j)
                    if j < 7:
                        top2[k] = top2[k] - m_top * c
                    low2[k] = low2[k] - m_low * c
            row = row_of(cur, j)
            cur = cur - m_top * row
            if not last:
                nxt = nxt - m_low * row
        pivot = top[0]
        for j in range(1, 8):
            pivot = jnp.where(sub == j, top[j], pivot)
        scale = lax.rsqrt(pivot)
        cur = cur * scale
        later = jnp.where(lane >= r0 + 8, cur, 0.0)
        out = later
        for k in range(8):
            out = jnp.where((lane == r0 + k) & (sub <= k), top[k] * scale, out)
        a_ref[r0 : r0 + 8, :] = out
        e_ref[r0 : r0 + 8, :] = jnp.where(lane < r0 + 8, cur, 0.0)
        if not last:
            work[s + 1] = nxt
            top = low2
        if s + 2 < strips:
            update = outer_product(later, cur)
            for t in range(s + 2, strips):
                work[t] = jnp.where(here, 0.0, work[t]) - update[8 * t : 8 * t + 8, :]


def cholesky_kernel(
    scale, core, mine_ref, other_ref, out_ref, u_ref, g_ref, a_ref, e_ref, s_ref, in_sem, out_sem
):
    me = core[0]
    size = u_ref.shape[0]
    nb = size // TILE
    early = nb
    pieces = ((0, early), (early, g_ref.shape[1]))

    def loads(k):
        lo, hi = pieces[k]
        return (
            pltpu.make_async_copy(mine_ref.at[lo:hi], g_ref.at[me, lo:hi], in_sem.at[2 * k]),
            pltpu.make_async_copy(
                other_ref.at[lo:hi], g_ref.at[1 - me, lo:hi], in_sem.at[2 * k + 1]
            ),
        )

    def store(k):
        rows = slice(TILE * k, TILE * (k + 1))
        return pltpu.make_async_copy(u_ref.at[rows], out_ref.at[rows], out_sem.at[k])

    for k in range(2):
        for copy in loads(k):
            copy.start()

    def body(i, carry):
        for k in range(nb):
            h = k % 2
            r0 = TILE * (k - h)
            c0 = TILE * k

            @pl.when(i == k)
            def _(k=k, h=h, r0=r0, c0=c0):
                if k == 0 or k == 2:
                    for copy in loads(k // 2):
                        copy.wait()
                if h == 0:
                    for hh in range(2):
                        for j in range(k + hh, nb):
                            idx = block_index(nb, k + hh, j)
                            s_ref[TILE * hh : TILE * (hh + 1), TILE * j : TILE * (j + 1)] = (
                                g_ref[idx % CORES, idx // CORES] * scale
                            )
                        if r0:
                            first = c0 + TILE * hh
                            s_ref[TILE * hh : TILE * (hh + 1), first:] -= dot_tn(
                                u_ref[0:r0, first : first + TILE], u_ref[0:r0, first:]
                            )
                else:
                    s_ref[TILE:, c0:] -= dot_tn(u_ref[r0:c0, c0 : c0 + TILE], u_ref[r0:c0, c0:])
                a_ref[...] = s_ref[TILE * h : TILE * (h + 1), c0 : c0 + TILE]

        factor_block(a_ref, e_ref)
        for k in range(nb):
            h = k % 2
            c0 = TILE * k

            @pl.when(i == k)
            def _(k=k, h=h, c0=c0):
                rows = slice(c0, c0 + TILE)
                if c0:
                    u_ref[rows, 0:c0] = jnp.zeros((TILE, c0), jnp.float32)
                u_ref[rows, c0 : c0 + TILE] = a_ref[...]
                if c0 + TILE < size:
                    u_ref[rows, c0 + TILE :] = dot_nn(
                        e_ref[...], s_ref[TILE * h : TILE * (h + 1), c0 + TILE :]
                    )
                store(k).start()

        return carry

    lax.fori_loop(0, nb, body, 0)
    for k in range(nb):
        store(k).wait()


def cholesky_blocks(core, mine, other, size, scale):
    half = mine.shape[0]
    anywhere = pl.BlockSpec(memory_space=pl.ANY)
    return pl.pallas_call(
        functools.partial(cholesky_kernel, scale),
        out_shape=jax.ShapeDtypeStruct((size, size), jnp.float32),
        grid_spec=pltpu.PrefetchScalarGridSpec(
            num_scalar_prefetch=1,
            grid=(1,),
            in_specs=[anywhere, anywhere],
            out_specs=anywhere,
            scratch_shapes=[
                pltpu.VMEM((size, size), jnp.float32),
                pltpu.VMEM((CORES, half, TILE, TILE), jnp.float32),
                pltpu.VMEM((TILE, TILE), jnp.float32),
                pltpu.VMEM((TILE, TILE), jnp.float32),
                pltpu.VMEM((2 * TILE, size), jnp.float32),
                pltpu.SemaphoreType.DMA((4,)),
                pltpu.SemaphoreType.DMA((size // TILE,)),
            ],
        ),
        compiler_params=pltpu.CompilerParams(vmem_limit_bytes=VMEM_BYTES),
        name="cholesky",
    )(core, mine, other)


def swap_cores(x):
    return lax.ppermute(x, "core", [(0, 1), (1, 0)])


def gather_plane(x):
    plane = lax.axis_size(PLANE_AXES)
    copies = jnp.broadcast_to(x[None], (plane, *x.shape))
    return lax.all_to_all(copies, PLANE_AXES, split_axis=0, concat_axis=0, tiled=True)


def shards(records, offsets, column_map, angles):
    parts = lax.axis_size(GAUGE_AXES)
    rows, cols_here = records.shape
    cols = column_map.shape[0]
    core = lax.axis_index("core").astype(jnp.int32).reshape(1)
    records_t = records.T
    arms = column_map.reshape(-1, TILE)
    angles = angles.reshape(-1, TILE)
    acc = None
    for filtered in filter_records(records_t, offsets, parts):
        regrouped = lax.all_to_all(filtered, GAUGE_AXES, split_axis=0, concat_axis=0, tiled=True)
        acc = gram_chunk(core, arms, regrouped.reshape(cols, -1), angles, acc)
    mine, other = acc
    half = mine.shape[0]
    mine = mine + swap_cores(other)
    plane = lax.axis_size(PLANE_AXES)
    share = half * TILE // plane
    spread = lax.all_to_all(
        mine.reshape(plane, share, TILE), PLANE_AXES, split_axis=0, concat_axis=0, tiled=True
    )
    mine = gather_plane(spread.sum(0)).reshape(half, TILE, TILE)
    other = swap_cores(mine)
    total = rows * lax.axis_size(SAMPLE_AXES)
    return cholesky_blocks(core, mine, other, cols, 1.0 / total)


def solution(mesh):
    devices = mesh.devices
    tm, gauge = devices.shape
    side = int(round(tm**0.5))
    fine = Mesh(
        devices.reshape(side, tm // side, gauge // CORES, CORES), SAMPLE_AXES + GAUGE_AXES
    )
    placed = (P(SAMPLE_AXES, GAUGE_AXES), P(SAMPLE_AXES), P(), P())
    return jax.shard_map(shards, mesh=fine, in_specs=placed, out_specs=P(), check_vma=False)
```

```python
import functools

import jax
import jax.numpy as jnp
from jax import lax
from jax.experimental import pallas as pl
from jax.experimental.pallas import tpu as pltpu
from jax.sharding import Mesh
from jax.sharding import PartitionSpec as P

BLOCK = 1024
BAND = 64
TILE = 128
CORES = 2
SAMPLE_AXES = ("z", "x")
GAUGE_AXES = ("y", "core")
PLANE_AXES = ("z", "x", "y")
HIGHEST = lax.Precision.HIGHEST
VMEM_BYTES = 56 * 1024 * 1024


def block_index(nb, i, j):
    return sum(nb - k for k in range(i)) + (j - i)


class Layout:
    def __init__(self, nb, plane):
        self.nb, self.plane = nb, plane
        self.used = nb * (nb + 1) // 2
        self.rows_early = nb // 3
        need = block_index(nb, self.rows_early, self.rows_early)
        step = max(1, 8 * plane // TILE)
        self.early = -(-(-(-need // CORES)) // step) * step
        self.half = -(-(-(-self.used // CORES)) // step) * step
        self.share = (self.early * TILE // plane, (self.half - self.early) * TILE // plane)

    def pieces(self, position):
        late = position >= self.early
        share = self.share[late]
        base = self.share[0] if late else 0
        row = (position - (self.early if late else 0)) * TILE
        at, out = 0, []
        while at < TILE:
            chip, inside = divmod(row + at, share)
            n = min(share - inside, TILE - at)
            out.append((at, chip, base + inside, n))
            at += n
        return out


def dot_nt(a, b):
    return lax.dot_general(a, b, (((1,), (1,)), ((), ())), preferred_element_type=jnp.float32)


def filter_kernel(offsets, x_ref, head_ref, tail_ref):
    parts, _, split = head_ref.shape
    blocks = x_ref.shape[1] // BLOCK // parts
    for b in range(parts * blocks):
        start = offsets[pl.program_id(0) * parts * blocks + b]
        x = x_ref[:, b * BLOCK : (b + 1) * BLOCK]
        sample = lax.broadcasted_iota(jnp.int32, (1, BLOCK), 1)
        inside = jnp.where((sample >= start) & (sample < start + BAND), 1.0, 0.0)
        mask = jnp.broadcast_to(inside.astype(jnp.bfloat16), (TILE, BLOCK))
        baseline = dot_nt(x, mask) * (1.0 / BAND)
        for t in range(0, BLOCK, TILE):
            value = (x[:, t : t + TILE].astype(jnp.float32) - baseline).astype(jnp.bfloat16)
            here = b % blocks * BLOCK + t
            if here < split:
                head_ref[b // blocks, :, here : here + TILE] = value
            else:
                tail_ref[b // blocks, :, here - split : here - split + TILE] = value


def filter_records(records_t, offsets, parts):
    rows, samples = records_t.shape
    each = samples // parts
    tail = BLOCK // 2
    widths = (each - tail, tail)
    per = 2
    return pl.pallas_call(
        filter_kernel,
        out_shape=tuple(jax.ShapeDtypeStruct((parts, rows, w), jnp.bfloat16) for w in widths),
        grid_spec=pltpu.PrefetchScalarGridSpec(
            num_scalar_prefetch=1,
            grid=(parts // per,),
            in_specs=[pl.BlockSpec((rows, per * each), lambda d, off: (0, d))],
            out_specs=tuple(
                pl.BlockSpec((per, rows, w), lambda d, off: (d, 0, 0)) for w in widths
            ),
        ),
        compiler_params=pltpu.CompilerParams(vmem_limit_bytes=VMEM_BYTES),
        name="drift_filter",
    )(offsets, records_t)


def gram_kernel(layout, first, core, *refs):
    if first:
        map_ref, ft_ref, angle_ref, mine_out, other_out, rt_ref, acc_ref, sem = refs
        mine_in = other_in = None
    else:
        map_ref, ft_ref, angle_ref, mine_in, other_in, mine_out, other_out, rt_ref, acc_ref, sem = refs
    step = pl.program_id(0)
    me = core[0]

    def loads():
        return (
            pltpu.make_async_copy(mine_in, acc_ref.at[me], sem.at[0]),
            pltpu.make_async_copy(other_in, acc_ref.at[1 - me], sem.at[1]),
        )

    if not first:

        @pl.when(step == 0)
        def _():
            for copy in loads():
                copy.start()

    ft = ft_ref[...]
    cols, samples = ft.shape
    lanes = map_ref.shape[1]
    steps = pl.num_programs(0)

    def down(row):
        return jnp.broadcast_to(row, (lanes, lanes)).T

    def arm(k):
        source = down(map_ref[pl.ds(k * steps + step, 1), :].astype(jnp.float32))
        index = lax.broadcasted_iota(jnp.int32, (lanes, lanes), 1).astype(jnp.float32)
        pick = [jnp.where(source - c == index, 1.0, 0.0) for c in range(0, cols, lanes)]
        pick = jnp.concatenate(pick, axis=1).astype(jnp.bfloat16)
        return jnp.dot(pick, ft, preferred_element_type=jnp.float32)

    first_arm, middle_arm, last_arm = (arm(k) for k in range(3))
    shear = 2.0 * middle_arm - first_arm - last_arm
    angle = angle_ref[pl.ds(step, 1), :]
    cosine, sine = jnp.cos(angle), jnp.sin(angle)
    cos_sq, sin_sq, mixed = (
        jnp.tile(down(c), (1, samples // lanes))
        for c in (cosine * cosine, sine * sine, sine * cosine)
    )
    twist = shear * mixed
    along_x = first_arm * cos_sq + last_arm * sin_sq + twist
    along_y = first_arm * sin_sq + last_arm * cos_sq - twist
    shear_new = 2.0 * (last_arm - first_arm) * mixed + shear * (cos_sq - sin_sq)
    per_arm = rt_ref.shape[0] // 3
    here = pl.multiple_of(step * lanes, lanes)
    for k, value in enumerate((along_x, along_y, shear_new)):
        rt_ref[pl.ds(k * per_arm + here, lanes), :] = value.astype(jnp.bfloat16)

    @pl.when(step == pl.num_programs(0) - 1)
    def _():
        if not first:
            for copy in loads():
                copy.wait()
        nb = layout.nb

        def add(idx, block):
            for at, chip, row, n in layout.pieces(idx // CORES):
                here = (idx % CORES, chip, slice(row, row + n))
                if first:
                    acc_ref[here] = block[at : at + n]
                else:
                    acc_ref[here] += block[at : at + n]

        if first:
            for idx in range(layout.used, CORES * layout.half):
                add(idx, jnp.zeros((TILE, TILE), jnp.float32))
        for j in range(0, nb, 2):
            part = dot_nt(rt_ref[0 : TILE * (j + 2), :], rt_ref[TILE * j : TILE * (j + 2), :])
            for i in range(j + 2):
                for jj in range(max(i, j), j + 2):
                    cut = slice(TILE * (jj - j), TILE * (jj - j + 1))
                    add(block_index(nb, i, jj), part[TILE * i : TILE * (i + 1), cut])
        stores = (
            pltpu.make_async_copy(acc_ref.at[me], mine_out, sem.at[0]),
            pltpu.make_async_copy(acc_ref.at[1 - me], other_out, sem.at[1]),
        )
        for copy in stores:
            copy.start()
        for copy in stores:
            copy.wait()


def gram_chunk(layout, core, arms, ft, angles, so_far):
    cols, samples = ft.shape
    run = (layout.plane, sum(layout.share), TILE)
    shape = jax.ShapeDtypeStruct(run, jnp.float32)
    anywhere = pl.BlockSpec(memory_space=pl.ANY)
    return pl.pallas_call(
        functools.partial(gram_kernel, layout, so_far is None),
        out_shape=(shape, shape),
        grid_spec=pltpu.PrefetchScalarGridSpec(
            num_scalar_prefetch=1,
            grid=(angles.shape[0],),
            in_specs=[
                pl.BlockSpec(arms.shape, lambda g, core: (0, 0)),
                pl.BlockSpec((cols, samples), lambda g, core: (0, 0)),
                pl.BlockSpec(angles.shape, lambda g, core: (0, 0)),
            ]
            + ([] if so_far is None else [anywhere, anywhere]),
            out_specs=(anywhere, anywhere),
            scratch_shapes=[
                pltpu.VMEM((cols, samples), jnp.bfloat16),
                pltpu.VMEM((CORES, *run), jnp.float32),
                pltpu.SemaphoreType.DMA((2,)),
            ],
        ),
        compiler_params=pltpu.CompilerParams(vmem_limit_bytes=VMEM_BYTES),
        name="rotate_gram",
    )(core, arms, ft, angles, *(() if so_far is None else so_far))


def split3(x):
    high = x.astype(jnp.bfloat16).astype(jnp.float32)
    rest = x - high
    middle = rest.astype(jnp.bfloat16).astype(jnp.float32)
    return high, middle, rest - middle


def outer_product(a, b):
    a1, a2, a3 = split3(a)
    b1, b2, b3 = split3(b)
    left = jnp.concatenate([a1, a1, a2, a2, a1, a3], axis=0).astype(jnp.bfloat16)
    right = jnp.concatenate([b1, b2, b1, b2, b3, b1], axis=0).astype(jnp.bfloat16)
    return lax.dot_general(
        left, right, (((0,), (0,)), ((), ())), preferred_element_type=jnp.float32
    )


def factor_block(a_ref, e_ref):
    lane = lax.broadcasted_iota(jnp.int32, (8, TILE), 1)
    sub = lax.broadcasted_iota(jnp.int32, (8, TILE), 0)
    strips = TILE // 8
    work = [a_ref[8 * t : 8 * t + 8, :] for t in range(strips)]

    def columns(x, r0):
        return [jnp.broadcast_to(x[:, r0 + j : r0 + j + 1], (8, TILE)) for j in range(8)]

    def row_of(x, j):
        return jnp.broadcast_to(x[j : j + 1, :], (8, TILE))

    top = columns(work[0], 0)
    for s in range(strips):
        r0 = 8 * s
        below = strips - 1 - s
        here = (lane >= r0) & (lane < r0 + 8)
        cur = jnp.where(here, jnp.where(lane == r0 + sub, 1.0, 0.0), work[s])
        if below:
            low = columns(work[s + 1], r0)
            top2 = columns(work[s], r0 + 8)
            low2 = columns(work[s + 1], r0 + 8)
            nxt = jnp.where(here, 0.0, work[s + 1])
        if below > 1:
            third = columns(work[s + 2], r0)
            nxt2 = jnp.where(here, 0.0, work[s + 2])
        for j in range(8):
            inv = 1.0 / row_of(top[j], j)
            m_top = jnp.where(sub > j, top[j] * inv, 0.0)
            m_low = low[j] * inv if below else None
            m_third = third[j] * inv if below > 1 else None
            for k in range(j + 1, 8):
                c = row_of(top[k], j)
                if k == j + 1:
                    top[k] = top[k] - jnp.where(sub > j, top[j] * c, 0.0) * inv
                else:
                    top[k] = top[k] - m_top * c
                if below:
                    low[k] = low[k] - m_low * c
                if below > 1:
                    third[k] = third[k] - m_third * c
            if below:
                for k in range(8):
                    c = row_of(top2[k], j)
                    if j < 7:
                        top2[k] = top2[k] - m_top * c
                    low2[k] = low2[k] - m_low * c
            row = row_of(cur, j)
            cur = cur - m_top * row
            if below:
                nxt = nxt - m_low * row
            if below > 1:
                nxt2 = nxt2 - m_third * row
        pivot = top[0]
        for j in range(1, 8):
            pivot = jnp.where(sub == j, top[j], pivot)
        scale = lax.rsqrt(pivot)
        cur = cur * scale
        later = jnp.where(lane >= r0 + 8, cur, 0.0)
        out = later
        for k in range(8):
            out = jnp.where((lane == r0 + k) & (sub <= k), top[k] * scale, out)
        a_ref[r0 : r0 + 8, :] = out
        e_ref[r0 : r0 + 8, :] = jnp.where(lane < r0 + 8, cur, 0.0)
        if below:
            work[s + 1] = nxt
            top = low2
        if below > 1:
            work[s + 2] = nxt2
        if below > 2:
            update = outer_product(later, cur)
            for t in range(s + 3, strips):
                work[t] = jnp.where(here, 0.0, work[t]) - update[8 * t : 8 * t + 8, :]


def dot_parts(a, b, contract):
    return lax.dot_general(
        a, b, (((contract,), (0,)), ((), ())), preferred_element_type=jnp.float32
    )


def product(left, right, contract):
    m = left[0].shape[1 - contract]
    p = dot_parts(jnp.concatenate(left, axis=1 - contract), right[0], contract)
    q = dot_parts(jnp.concatenate(left[:2], axis=1 - contract), right[1], contract)
    r = dot_parts(left[0], right[2], contract)
    return p[:m] + ((p[m : 2 * m] + q[:m]) + ((p[2 * m :] + q[m:]) + r))


def parts3(x):
    return [v.astype(jnp.bfloat16) for v in split3(x)]


def cholesky_kernel(layout, scale, begin, end, core, *refs):
    sources = refs[: 2 if begin == 0 else 5]
    out_ref, u_ref, g_ref, a_ref, e_ref, s_ref, p_ref, in_sem, out_sem = refs[len(sources) :]
    me = core[0]
    size = u_ref.shape[0]
    nb, early = layout.nb, layout.early
    below = slice(0, TILE * begin)

    def part_loads(pair, lo, hi, to, sems):
        mine, other = pair
        n = hi - lo
        return [
            pltpu.make_async_copy(mine.at[lo:hi], g_ref.at[me, to : to + n], in_sem.at[sems]),
            pltpu.make_async_copy(
                other.at[lo:hi], g_ref.at[1 - me, to : to + n], in_sem.at[sems + 1]
            ),
        ]

    if begin == 0:
        first = block_index(nb, 2, 2) // CORES + 1
        now = part_loads(sources[:2], 0, first, 0, 0)
        later = part_loads(sources[:2], first, early, first, 2)
    else:
        first = block_index(nb, begin, begin) // CORES
        now = part_loads(sources[:2], first, early, first, 0)
        now += part_loads(sources[2:4], 0, layout.half - early, early, 2)
        now.append(pltpu.make_async_copy(sources[4].at[below], u_ref.at[below], in_sem.at[4]))
        later = []

    def store(k):
        rows = slice(TILE * k, TILE * (k + 1))
        return pltpu.make_async_copy(u_ref.at[rows], out_ref.at[rows], out_sem.at[k])

    for copy in now + later:
        copy.start()
    for copy in now:
        copy.wait()
    if begin:
        rest = slice(TILE * begin, size)
        for q, v in enumerate(parts3(u_ref[below, rest])):
            p_ref[q, below, rest] = v

    def up(rows, cols):
        return [p_ref[q, rows, cols] for q in range(3)]

    def body(i, carry):
        for k in range(begin, end):
            h = k % 2
            r0 = TILE * (k - h)
            c0 = TILE * k

            @pl.when(i == k)
            def _(k=k, h=h, r0=r0, c0=c0):
                if k == 2:
                    for copy in later:
                        copy.wait()
                if h == 0:
                    for hh in range(2):
                        for j in range(k, nb):
                            if j < k + hh:
                                block = jnp.zeros((TILE, TILE), jnp.float32)
                            else:
                                idx = block_index(nb, k + hh, j)
                                block = g_ref[idx % CORES, idx // CORES] * scale
                            s_ref[TILE * hh : TILE * (hh + 1), TILE * j : TILE * (j + 1)] = block
                    if r0:
                        panel = slice(r0, r0 + 2 * TILE)
                        s_ref[:, r0:] -= product(
                            up(slice(0, r0), panel), up(slice(0, r0), slice(r0, size)), 0
                        )
                else:
                    above = slice(r0, c0)
                    s_ref[TILE:, c0:] -= product(
                        up(above, slice(c0, c0 + TILE)), up(above, slice(c0, size)), 0
                    )
                a_ref[...] = s_ref[TILE * h : TILE * (h + 1), c0 : c0 + TILE]

        factor_block(a_ref, e_ref)
        for k in range(begin, end):
            h = k % 2
            c0 = TILE * k

            @pl.when(i == k)
            def _(k=k, h=h, c0=c0):
                rows = slice(c0, c0 + TILE)
                if c0:
                    u_ref[rows, 0:c0] = jnp.zeros((TILE, c0), jnp.float32)
                u_ref[rows, c0 : c0 + TILE] = a_ref[...]
                if c0 + TILE < size:
                    rest = slice(c0 + TILE, size)
                    solved = product(
                        parts3(e_ref[...]), parts3(s_ref[TILE * h : TILE * (h + 1), rest]), 1
                    )
                    u_ref[rows, rest] = solved
                    for q, v in enumerate(parts3(solved)):
                        p_ref[q, rows, rest] = v
                store(k).start()

        return carry

    lax.fori_loop(begin, end, body, 0)
    for k in range(begin, end):
        store(k).wait()


def cholesky_rows(layout, core, groups, so_far, scale):
    size = layout.nb * TILE
    begin, end = (0, layout.rows_early) if so_far is None else (layout.rows_early, layout.nb)
    anywhere = pl.BlockSpec(memory_space=pl.ANY)
    sources = [x for pair in groups for x in pair] + ([] if so_far is None else [so_far])
    return pl.pallas_call(
        functools.partial(cholesky_kernel, layout, scale, begin, end),
        out_shape=jax.ShapeDtypeStruct((size, size), jnp.float32),
        grid_spec=pltpu.PrefetchScalarGridSpec(
            num_scalar_prefetch=1,
            grid=(1,),
            in_specs=[anywhere] * len(sources),
            out_specs=anywhere,
            scratch_shapes=[
                pltpu.VMEM((size, size), jnp.float32),
                pltpu.VMEM((CORES, layout.half, TILE, TILE), jnp.float32),
                pltpu.VMEM((TILE, TILE), jnp.float32),
                pltpu.VMEM((TILE, TILE), jnp.float32),
                pltpu.VMEM((2 * TILE, size), jnp.float32),
                pltpu.VMEM((3, size, size), jnp.bfloat16),
                pltpu.SemaphoreType.DMA((5,)),
                pltpu.SemaphoreType.DMA((layout.nb,)),
            ],
        ),
        input_output_aliases={} if so_far is None else {len(sources): 0},
        cost_estimate=pl.CostEstimate(
            flops=40 * (end - begin) * size**2 * TILE, transcendentals=0, bytes_accessed=12 * size**2
        ),
        compiler_params=pltpu.CompilerParams(vmem_limit_bytes=VMEM_BYTES),
        name="cholesky",
    )(core, *sources)


def swap_cores(x):
    return lax.ppermute(x, "core", [(0, 1), (1, 0)])


def gather_plane(x):
    plane = lax.axis_size(PLANE_AXES)
    copies = jnp.broadcast_to(x[None], (plane, *x.shape))
    return lax.all_to_all(copies, PLANE_AXES, split_axis=0, concat_axis=0, tiled=True)


def shards(records, offsets, column_map, angles):
    parts = lax.axis_size(GAUGE_AXES)
    rows, cols_here = records.shape
    cols = column_map.shape[0]
    core = lax.axis_index("core").astype(jnp.int32).reshape(1)
    records_t = records.T
    arms = column_map.reshape(-1, TILE)
    angles = angles.reshape(-1, TILE)
    layout = Layout(cols // TILE, lax.axis_size(PLANE_AXES))
    acc = None
    for filtered in filter_records(records_t, offsets, parts):
        regrouped = lax.all_to_all(filtered, GAUGE_AXES, split_axis=0, concat_axis=0, tiled=True)
        acc = gram_chunk(layout, core, arms, regrouped.reshape(cols, -1), angles, acc)
    mine, other = acc
    mine = mine + swap_cores(other)
    spread = lax.all_to_all(mine, PLANE_AXES, split_axis=0, concat_axis=0, tiled=True).sum(0)
    scale = 1.0 / (rows * lax.axis_size(SAMPLE_AXES))
    early, late = jnp.split(spread, [layout.share[0]])
    early = gather_plane(early)
    late, early = lax.optimization_barrier((late, early))
    late = gather_plane(late)
    early, late = (g.reshape(-1, TILE, TILE) for g in (early, late))
    groups = [(early, swap_cores(early))]
    upper = cholesky_rows(layout, core, groups, None, scale)
    late, upper = lax.optimization_barrier((late, upper))
    groups.append((late, swap_cores(late)))
    return cholesky_rows(layout, core, groups, upper, scale)


def solution(mesh):
    devices = mesh.devices
    tm, gauge = devices.shape
    side = int(round(tm**0.5))
    fine = Mesh(
        devices.reshape(side, tm // side, gauge // CORES, CORES), SAMPLE_AXES + GAUGE_AXES
    )
    placed = (P(SAMPLE_AXES, GAUGE_AXES), P(SAMPLE_AXES), P(), P())
    return jax.shard_map(shards, mesh=fine, in_specs=placed, out_specs=P(), check_vma=False)
```

```python
import functools

import jax
import jax.numpy as jnp
from jax import lax
from jax.experimental import pallas as pl
from jax.experimental.pallas import tpu as pltpu
from jax.sharding import Mesh
from jax.sharding import PartitionSpec as P

BLOCK = 1024
BAND = 64
TILE = 128
CORES = 2
SAMPLE_AXES = ("z", "x")
GAUGE_AXES = ("y", "core")
PLANE_AXES = ("z", "x", "y")
HIGHEST = lax.Precision.HIGHEST
VMEM_BYTES = 56 * 1024 * 1024


class Layout:
    def __init__(self, nb, plane):
        self.nb, self.plane = nb, plane
        self.lead = lead = nb * 2 // 3
        order = [(i, j) for i in range(lead) for j in range(i, lead)]
        self.leading = len(order)
        order += [(i, j) for i in range(nb) for j in range(max(i, lead), nb)]
        self.number = {ij: n for n, ij in enumerate(order)}
        self.used = len(order)
        step = max(1, 8 * plane // TILE)
        self.early = -(-(-(-self.leading // CORES)) // step) * step
        self.half = -(-(-(-self.used // CORES)) // step) * step
        self.share = (self.early * TILE // plane, (self.half - self.early) * TILE // plane)

    def pieces(self, position):
        late = position >= self.early
        share = self.share[late]
        base = self.share[0] if late else 0
        row = (position - (self.early if late else 0)) * TILE
        at, out = 0, []
        while at < TILE:
            chip, inside = divmod(row + at, share)
            n = min(share - inside, TILE - at)
            out.append((at, chip, base + inside, n))
            at += n
        return out


def dot_nt(a, b):
    return lax.dot_general(a, b, (((1,), (1,)), ((), ())), preferred_element_type=jnp.float32)


def filter_kernel(offsets, x_ref, head_ref, tail_ref):
    parts, _, split = head_ref.shape
    blocks = x_ref.shape[1] // BLOCK // parts
    for b in range(parts * blocks):
        start = offsets[pl.program_id(0) * parts * blocks + b]
        x = x_ref[:, b * BLOCK : (b + 1) * BLOCK]
        sample = lax.broadcasted_iota(jnp.int32, (1, BLOCK), 1)
        inside = jnp.where((sample >= start) & (sample < start + BAND), 1.0, 0.0)
        mask = jnp.broadcast_to(inside.astype(jnp.bfloat16), (TILE, BLOCK))
        baseline = dot_nt(x, mask) * (1.0 / BAND)
        for t in range(0, BLOCK, TILE):
            value = (x[:, t : t + TILE].astype(jnp.float32) - baseline).astype(jnp.bfloat16)
            here = b % blocks * BLOCK + t
            if here < split:
                head_ref[b // blocks, :, here : here + TILE] = value
            else:
                tail_ref[b // blocks, :, here - split : here - split + TILE] = value


def filter_records(records_t, offsets, parts):
    rows, samples = records_t.shape
    each = samples // parts
    tail = BLOCK // 2
    widths = (each - tail, tail)
    per = 2
    return pl.pallas_call(
        filter_kernel,
        out_shape=tuple(jax.ShapeDtypeStruct((parts, rows, w), jnp.bfloat16) for w in widths),
        grid_spec=pltpu.PrefetchScalarGridSpec(
            num_scalar_prefetch=1,
            grid=(parts // per,),
            in_specs=[pl.BlockSpec((rows, per * each), lambda d, off: (0, d))],
            out_specs=tuple(
                pl.BlockSpec((per, rows, w), lambda d, off: (d, 0, 0)) for w in widths
            ),
        ),
        compiler_params=pltpu.CompilerParams(vmem_limit_bytes=VMEM_BYTES),
        name="drift_filter",
    )(offsets, records_t)


def gram_kernel(layout, first, core, *refs):
    if first:
        map_ref, ft_ref, angle_ref, mine_out, other_out, rt_ref, acc_ref, sem = refs
        mine_in = other_in = None
    else:
        map_ref, ft_ref, angle_ref, mine_in, other_in, mine_out, other_out, rt_ref, acc_ref, sem = refs
    step = pl.program_id(0)
    me = core[0]

    def loads():
        return (
            pltpu.make_async_copy(mine_in, acc_ref.at[me], sem.at[0]),
            pltpu.make_async_copy(other_in, acc_ref.at[1 - me], sem.at[1]),
        )

    if not first:

        @pl.when(step == 0)
        def _():
            for copy in loads():
                copy.start()

    ft = ft_ref[...]
    cols, samples = ft.shape
    lanes = map_ref.shape[1]
    steps = pl.num_programs(0)

    def down(row):
        return jnp.broadcast_to(row, (lanes, lanes)).T

    def arm(k):
        source = down(map_ref[pl.ds(k * steps + step, 1), :].astype(jnp.float32))
        index = lax.broadcasted_iota(jnp.int32, (lanes, lanes), 1).astype(jnp.float32)
        pick = [jnp.where(source - c == index, 1.0, 0.0) for c in range(0, cols, lanes)]
        pick = jnp.concatenate(pick, axis=1).astype(jnp.bfloat16)
        return jnp.dot(pick, ft, preferred_element_type=jnp.float32)

    first_arm, middle_arm, last_arm = (arm(k) for k in range(3))
    shear = 2.0 * middle_arm - first_arm - last_arm
    angle = angle_ref[pl.ds(step, 1), :]
    cosine, sine = jnp.cos(angle), jnp.sin(angle)
    cos_sq, sin_sq, mixed = (
        jnp.tile(down(c), (1, samples // lanes))
        for c in (cosine * cosine, sine * sine, sine * cosine)
    )
    twist = shear * mixed
    along_x = first_arm * cos_sq + last_arm * sin_sq + twist
    along_y = first_arm * sin_sq + last_arm * cos_sq - twist
    shear_new = 2.0 * (last_arm - first_arm) * mixed + shear * (cos_sq - sin_sq)
    per_arm = rt_ref.shape[0] // 3
    here = pl.multiple_of(step * lanes, lanes)
    for k, value in enumerate((along_x, along_y, shear_new)):
        rt_ref[pl.ds(k * per_arm + here, lanes), :] = value.astype(jnp.bfloat16)

    @pl.when(step == pl.num_programs(0) - 1)
    def _():
        if not first:
            for copy in loads():
                copy.wait()
        nb = layout.nb

        def add(idx, block):
            for at, chip, row, n in layout.pieces(idx // CORES):
                here = (idx % CORES, chip, slice(row, row + n))
                if first:
                    acc_ref[here] = block[at : at + n]
                else:
                    acc_ref[here] += block[at : at + n]

        if first:
            for idx in range(layout.used, CORES * layout.half):
                add(idx, jnp.zeros((TILE, TILE), jnp.float32))
        for j in range(0, nb, 2):
            part = dot_nt(rt_ref[0 : TILE * (j + 2), :], rt_ref[TILE * j : TILE * (j + 2), :])
            for i in range(j + 2):
                for jj in range(max(i, j), j + 2):
                    cut = slice(TILE * (jj - j), TILE * (jj - j + 1))
                    add(layout.number[i, jj], part[TILE * i : TILE * (i + 1), cut])
        stores = (
            pltpu.make_async_copy(acc_ref.at[me], mine_out, sem.at[0]),
            pltpu.make_async_copy(acc_ref.at[1 - me], other_out, sem.at[1]),
        )
        for copy in stores:
            copy.start()
        for copy in stores:
            copy.wait()


def gram_chunk(layout, core, arms, ft, angles, so_far):
    cols, samples = ft.shape
    run = (layout.plane, sum(layout.share), TILE)
    shape = jax.ShapeDtypeStruct(run, jnp.float32)
    anywhere = pl.BlockSpec(memory_space=pl.ANY)
    return pl.pallas_call(
        functools.partial(gram_kernel, layout, so_far is None),
        out_shape=(shape, shape),
        grid_spec=pltpu.PrefetchScalarGridSpec(
            num_scalar_prefetch=1,
            grid=(angles.shape[0],),
            in_specs=[
                pl.BlockSpec(arms.shape, lambda g, core: (0, 0)),
                pl.BlockSpec((cols, samples), lambda g, core: (0, 0)),
                pl.BlockSpec(angles.shape, lambda g, core: (0, 0)),
            ]
            + ([] if so_far is None else [anywhere, anywhere]),
            out_specs=(anywhere, anywhere),
            scratch_shapes=[
                pltpu.VMEM((cols, samples), jnp.bfloat16),
                pltpu.VMEM((CORES, *run), jnp.float32),
                pltpu.SemaphoreType.DMA((2,)),
            ],
        ),
        compiler_params=pltpu.CompilerParams(vmem_limit_bytes=VMEM_BYTES),
        name="rotate_gram",
    )(core, arms, ft, angles, *(() if so_far is None else so_far))


def split3(x):
    high = x.astype(jnp.bfloat16).astype(jnp.float32)
    rest = x - high
    middle = rest.astype(jnp.bfloat16).astype(jnp.float32)
    return high, middle, rest - middle


def outer_product(a, b):
    a1, a2, a3 = split3(a)
    b1, b2, b3 = split3(b)
    left = jnp.concatenate([a1, a1, a2, a2, a1, a3], axis=0).astype(jnp.bfloat16)
    right = jnp.concatenate([b1, b2, b1, b2, b3, b1], axis=0).astype(jnp.bfloat16)
    return lax.dot_general(
        left, right, (((0,), (0,)), ((), ())), preferred_element_type=jnp.float32
    )


def factor_block(a_ref, e_ref):
    lane = lax.broadcasted_iota(jnp.int32, (8, TILE), 1)
    sub = lax.broadcasted_iota(jnp.int32, (8, TILE), 0)
    strips = TILE // 8
    work = [a_ref[8 * t : 8 * t + 8, :] for t in range(strips)]

    def columns(x, r0):
        return [jnp.broadcast_to(x[:, r0 + j : r0 + j + 1], (8, TILE)) for j in range(8)]

    def row_of(x, j):
        return jnp.broadcast_to(x[j : j + 1, :], (8, TILE))

    top = columns(work[0], 0)
    for s in range(strips):
        r0 = 8 * s
        below = strips - 1 - s
        here = (lane >= r0) & (lane < r0 + 8)
        cur = jnp.where(here, jnp.where(lane == r0 + sub, 1.0, 0.0), work[s])
        if below:
            low = columns(work[s + 1], r0)
            top2 = columns(work[s], r0 + 8)
            low2 = columns(work[s + 1], r0 + 8)
            nxt = jnp.where(here, 0.0, work[s + 1])
        if below > 1:
            third = columns(work[s + 2], r0)
            nxt2 = jnp.where(here, 0.0, work[s + 2])
        for j in range(8):
            inv = 1.0 / row_of(top[j], j)
            m_top = jnp.where(sub > j, top[j] * inv, 0.0)
            m_low = low[j] * inv if below else None
            m_third = third[j] * inv if below > 1 else None
            for k in range(j + 1, 8):
                c = row_of(top[k], j)
                if k == j + 1:
                    top[k] = top[k] - jnp.where(sub > j, top[j] * c, 0.0) * inv
                else:
                    top[k] = top[k] - m_top * c
                if below:
                    low[k] = low[k] - m_low * c
                if below > 1:
                    third[k] = third[k] - m_third * c
            if below:
                for k in range(8):
                    c = row_of(top2[k], j)
                    if j < 7:
                        top2[k] = top2[k] - m_top * c
                    low2[k] = low2[k] - m_low * c
            row = row_of(cur, j)
            cur = cur - m_top * row
            if below:
                nxt = nxt - m_low * row
            if below > 1:
                nxt2 = nxt2 - m_third * row
        pivot = top[0]
        for j in range(1, 8):
            pivot = jnp.where(sub == j, top[j], pivot)
        scale = lax.rsqrt(pivot)
        cur = cur * scale
        later = jnp.where(lane >= r0 + 8, cur, 0.0)
        out = later
        for k in range(8):
            out = jnp.where((lane == r0 + k) & (sub <= k), top[k] * scale, out)
        a_ref[r0 : r0 + 8, :] = out
        e_ref[r0 : r0 + 8, :] = jnp.where(lane < r0 + 8, cur, 0.0)
        if below:
            work[s + 1] = nxt
            top = low2
        if below > 1:
            work[s + 2] = nxt2
        if below > 2:
            update = outer_product(later, cur)
            for t in range(s + 3, strips):
                work[t] = jnp.where(here, 0.0, work[t]) - update[8 * t : 8 * t + 8, :]


def dot_parts(a, b, contract):
    return lax.dot_general(
        a, b, (((contract,), (0,)), ((), ())), preferred_element_type=jnp.float32
    )


def product(left, right, contract):
    if left[0].shape[contract] <= TILE:
        pairs = ((0, 0), (0, 1), (1, 0), (1, 1), (0, 2), (2, 0))
        return dot_parts(
            jnp.concatenate([left[p] for p, _ in pairs], axis=contract),
            jnp.concatenate([right[q] for _, q in pairs], axis=0),
            contract,
        )
    m = left[0].shape[1 - contract]
    p = dot_parts(jnp.concatenate(left, axis=1 - contract), right[0], contract)
    q = dot_parts(jnp.concatenate(left[:2], axis=1 - contract), right[1], contract)
    r = dot_parts(left[0], right[2], contract)
    return p[:m] + ((p[m : 2 * m] + q[:m]) + ((p[2 * m :] + q[m:]) + r))


def parts3(x):
    return [v.astype(jnp.bfloat16) for v in split3(x)]


def cholesky_kernel(layout, scale, leading, core, *refs):
    n_in = 2 if leading else 6
    sources, refs = refs[:n_in], refs[n_in:]
    out_ref, refs = refs[0], refs[1:]
    if leading:
        inverse_ref, refs = refs[0], refs[1:]
    u_ref, g_ref, a_ref, e_ref, s_ref, p_ref, i_ref, in_sem, out_sem = refs
    me = core[0]
    nb, lead, early = layout.nb, layout.lead, layout.early
    begin, end = (0, lead) if leading else (lead, nb)
    edge = TILE * lead
    size = edge if leading else TILE * nb
    square = (slice(0, edge), slice(0, edge))
    corner = (slice(0, edge), slice(edge, TILE * nb))

    def part_loads(pair, lo, hi, to, sems):
        mine, other = pair
        n = hi - lo
        return [
            pltpu.make_async_copy(mine.at[lo:hi], g_ref.at[me, to : to + n], in_sem.at[sems]),
            pltpu.make_async_copy(
                other.at[lo:hi], g_ref.at[1 - me, to : to + n], in_sem.at[sems + 1]
            ),
        ]

    if leading:
        loads = part_loads(sources[:2], 0, early, 0, 0)
    else:
        first = layout.leading // CORES
        loads = part_loads(sources[2:4], 0, layout.half - early, early, 2)
        if first < early:
            loads += part_loads(sources[:2], first, early, first, 0)
        loads.append(pltpu.make_async_copy(sources[4].at[square], u_ref.at[square], in_sem.at[4]))
        loads.append(pltpu.make_async_copy(sources[5], i_ref, in_sem.at[5]))

    def store(k):
        here = (slice(TILE * k, TILE * (k + 1)), slice(0, size))
        return pltpu.make_async_copy(u_ref.at[here], out_ref.at[here], out_sem.at[k])

    def gram(i, j):
        n = layout.number[i, j]
        return g_ref[n % CORES, n // CORES] * scale

    def up(rows, cols):
        return [p_ref[q, rows, cols] for q in range(3)]

    def keep(rows, cols, value):
        for q, v in enumerate(parts3(value)):
            p_ref[q, rows, cols] = v

    for copy in loads:
        copy.start()
    for copy in loads:
        copy.wait()

    stores = []
    if not leading:
        right = slice(edge, size)
        for k in range(lead):
            rows, cols = slice(TILE * k, TILE * (k + 1)), slice(TILE * k, edge)
            keep(rows, cols, u_ref[rows, cols])
        for k in range(lead):
            rows = slice(TILE * k, TILE * (k + 1))
            above = slice(0, TILE * k)
            value = jnp.concatenate([gram(k, j) for j in range(lead, nb)], axis=1)
            if k:
                value = value - product(up(above, rows), up(above, right), 0)
            value = product(parts3(i_ref[k]), parts3(value), 1)
            u_ref[rows, right] = value
            keep(rows, right, value)
        stores.append(
            pltpu.make_async_copy(u_ref.at[corner], out_ref.at[corner], out_sem.at[0])
        )
        stores[0].start()

    def body(i, carry):
        for k in range(begin, end):
            h = k % 2
            r0 = TILE * (k - h)
            c0 = TILE * k

            @pl.when(i == k)
            def _(k=k, h=h, r0=r0, c0=c0):
                if h == 0:
                    for hh in range(2):
                        for j in range(k, size // TILE):
                            if j < k + hh:
                                block = jnp.zeros((TILE, TILE), jnp.float32)
                            else:
                                block = gram(k + hh, j)
                            s_ref[TILE * hh : TILE * (hh + 1), TILE * j : TILE * (j + 1)] = block
                    if r0:
                        panel = slice(r0, r0 + 2 * TILE)
                        s_ref[:, r0:size] -= product(
                            up(slice(0, r0), panel), up(slice(0, r0), slice(r0, size)), 0
                        )
                else:
                    above = slice(r0, c0)
                    s_ref[TILE:, c0:size] -= product(
                        up(above, slice(c0, c0 + TILE)), up(above, slice(c0, size)), 0
                    )
                a_ref[...] = s_ref[TILE * h : TILE * (h + 1), c0 : c0 + TILE]

        factor_block(a_ref, e_ref)
        for k in range(begin, end):
            h = k % 2
            c0 = TILE * k

            @pl.when(i == k)
            def _(k=k, h=h, c0=c0):
                rows = slice(c0, c0 + TILE)
                if c0:
                    u_ref[rows, 0:c0] = jnp.zeros((TILE, c0), jnp.float32)
                u_ref[rows, c0 : c0 + TILE] = a_ref[...]
                if leading:
                    i_ref[k] = e_ref[...]
                if c0 + TILE < size:
                    rest = slice(c0 + TILE, size)
                    solved = product(
                        parts3(e_ref[...]), parts3(s_ref[TILE * h : TILE * (h + 1), rest]), 1
                    )
                    u_ref[rows, rest] = solved
                    keep(rows, rest, solved)
                store(k).start()

        return carry

    lax.fori_loop(begin, end, body, 0)
    if leading:
        stores.append(pltpu.make_async_copy(i_ref, inverse_ref, in_sem.at[4]))
        stores[0].start()
    stores += [store(k) for k in range(begin, end)]
    for copy in stores:
        copy.wait()


def cholesky_part(layout, core, groups, so_far, scale):
    size = layout.nb * TILE
    leading = so_far is None
    anywhere = pl.BlockSpec(memory_space=pl.ANY)
    sources = [x for pair in groups for x in pair] + ([] if leading else list(so_far))
    factor = jax.ShapeDtypeStruct((size, size), jnp.float32)
    inverses = jax.ShapeDtypeStruct((layout.lead, TILE, TILE), jnp.float32)
    blocks = layout.lead if leading else layout.nb - layout.lead
    return pl.pallas_call(
        functools.partial(cholesky_kernel, layout, scale, leading),
        out_shape=(factor, inverses) if leading else factor,
        grid_spec=pltpu.PrefetchScalarGridSpec(
            num_scalar_prefetch=1,
            grid=(1,),
            in_specs=[anywhere] * len(sources),
            out_specs=(anywhere, anywhere) if leading else anywhere,
            scratch_shapes=[
                pltpu.VMEM((size, size), jnp.float32),
                pltpu.VMEM((CORES, layout.half, TILE, TILE), jnp.float32),
                pltpu.VMEM((TILE, TILE), jnp.float32),
                pltpu.VMEM((TILE, TILE), jnp.float32),
                pltpu.VMEM((2 * TILE, size), jnp.float32),
                pltpu.VMEM((3, size, size), jnp.bfloat16),
                pltpu.VMEM((layout.lead, TILE, TILE), jnp.float32),
                pltpu.SemaphoreType.DMA((6,)),
                pltpu.SemaphoreType.DMA((layout.nb,)),
            ],
        ),
        input_output_aliases={} if leading else {len(sources) - 1: 0},
        cost_estimate=pl.CostEstimate(
            flops=40 * blocks * size**2 * TILE, transcendentals=0, bytes_accessed=12 * size**2
        ),
        compiler_params=pltpu.CompilerParams(vmem_limit_bytes=VMEM_BYTES),
        name="cholesky",
    )(core, *sources)


def swap_cores(x):
    return lax.ppermute(x, "core", [(0, 1), (1, 0)])


def gather_plane(x):
    plane = lax.axis_size(PLANE_AXES)
    copies = jnp.broadcast_to(x[None], (plane, *x.shape))
    return lax.all_to_all(copies, PLANE_AXES, split_axis=0, concat_axis=0, tiled=True)


def shards(records, offsets, column_map, angles):
    parts = lax.axis_size(GAUGE_AXES)
    rows, cols_here = records.shape
    cols = column_map.shape[0]
    core = lax.axis_index("core").astype(jnp.int32).reshape(1)
    records_t = records.T
    arms = column_map.reshape(-1, TILE)
    angles = angles.reshape(-1, TILE)
    layout = Layout(cols // TILE, lax.axis_size(PLANE_AXES))
    acc = None
    for filtered in filter_records(records_t, offsets, parts):
        regrouped = lax.all_to_all(filtered, GAUGE_AXES, split_axis=0, concat_axis=0, tiled=True)
        acc = gram_chunk(layout, core, arms, regrouped.reshape(cols, -1), angles, acc)
    mine, other = acc
    mine = mine + swap_cores(other)
    spread = lax.all_to_all(mine, PLANE_AXES, split_axis=0, concat_axis=0, tiled=True).sum(0)
    scale = 1.0 / (rows * lax.axis_size(SAMPLE_AXES))
    early, late = jnp.split(spread, [layout.share[0]])
    early = gather_plane(early)
    late, early = lax.optimization_barrier((late, early))
    late = gather_plane(late)
    early, late = (g.reshape(-1, TILE, TILE) for g in (early, late))
    groups = [(early, swap_cores(early))]
    upper, inverses = cholesky_part(layout, core, groups, None, scale)
    late, upper = lax.optimization_barrier((late, upper))
    groups.append((late, swap_cores(late)))
    return cholesky_part(layout, core, groups, (upper, inverses), scale)


def solution(mesh):
    devices = mesh.devices
    tm, gauge = devices.shape
    side = int(round(tm**0.5))
    fine = Mesh(
        devices.reshape(side, tm // side, gauge // CORES, CORES), SAMPLE_AXES + GAUGE_AXES
    )
    placed = (P(SAMPLE_AXES, GAUGE_AXES), P(SAMPLE_AXES), P(), P())
    return jax.shard_map(shards, mesh=fine, in_specs=placed, out_specs=P(), check_vma=False)
```

```python
import functools

import jax
import jax.numpy as jnp
from jax import lax
from jax.experimental import pallas as pl
from jax.experimental.pallas import tpu as pltpu
from jax.sharding import Mesh
from jax.sharding import PartitionSpec as P

BLOCK = 1024
BAND = 64
TILE = 128
CORES = 2
SAMPLE_AXES = ("z", "x")
GAUGE_AXES = ("y", "core")
PLANE_AXES = ("z", "x", "y")
HIGHEST = lax.Precision.HIGHEST
VMEM_BYTES = 56 * 1024 * 1024


class Layout:
    def __init__(self, nb, plane):
        self.nb, self.plane = nb, plane
        self.lead = lead = nb // 4 * 2
        order = [(i, j) for i in range(lead) for j in range(i, lead)]
        self.leading = len(order)
        order += [(i, j) for i in range(nb) for j in range(max(i, lead), nb)]
        self.number = {ij: n for n, ij in enumerate(order)}
        self.used = len(order)
        step = max(1, 8 * plane // TILE)
        self.early = -(-(-(-self.leading // CORES)) // step) * step
        self.half = -(-(-(-self.used // CORES)) // step) * step
        self.share = (self.early * TILE // plane, (self.half - self.early) * TILE // plane)

    def pieces(self, position):
        late = position >= self.early
        share = self.share[late]
        base = self.share[0] if late else 0
        row = (position - (self.early if late else 0)) * TILE
        at, out = 0, []
        while at < TILE:
            chip, inside = divmod(row + at, share)
            n = min(share - inside, TILE - at)
            out.append((at, chip, base + inside, n))
            at += n
        return out


def dot_nt(a, b):
    return lax.dot_general(a, b, (((1,), (1,)), ((), ())), preferred_element_type=jnp.float32)


def filter_kernel(offsets, x_ref, head_ref, tail_ref):
    parts, _, split = head_ref.shape
    blocks = x_ref.shape[1] // BLOCK // parts
    for b in range(parts * blocks):
        start = offsets[pl.program_id(0) * parts * blocks + b]
        x = x_ref[:, b * BLOCK : (b + 1) * BLOCK]
        sample = lax.broadcasted_iota(jnp.int32, (1, BLOCK), 1)
        inside = jnp.where((sample >= start) & (sample < start + BAND), 1.0, 0.0)
        mask = jnp.broadcast_to(inside.astype(jnp.bfloat16), (TILE, BLOCK))
        baseline = dot_nt(x, mask) * (1.0 / BAND)
        for t in range(0, BLOCK, TILE):
            value = (x[:, t : t + TILE].astype(jnp.float32) - baseline).astype(jnp.bfloat16)
            here = b % blocks * BLOCK + t
            if here < split:
                head_ref[b // blocks, :, here : here + TILE] = value
            else:
                tail_ref[b // blocks, :, here - split : here - split + TILE] = value


def filter_records(records_t, offsets, parts):
    rows, samples = records_t.shape
    each = samples // parts
    tail = BLOCK // 2
    widths = (each - tail, tail)
    per = 2
    return pl.pallas_call(
        filter_kernel,
        out_shape=tuple(jax.ShapeDtypeStruct((parts, rows, w), jnp.bfloat16) for w in widths),
        grid_spec=pltpu.PrefetchScalarGridSpec(
            num_scalar_prefetch=1,
            grid=(parts // per,),
            in_specs=[pl.BlockSpec((rows, per * each), lambda d, off: (0, d))],
            out_specs=tuple(
                pl.BlockSpec((per, rows, w), lambda d, off: (d, 0, 0)) for w in widths
            ),
        ),
        compiler_params=pltpu.CompilerParams(vmem_limit_bytes=VMEM_BYTES),
        name="drift_filter",
    )(offsets, records_t)


def gram_kernel(layout, first, core, *refs):
    if first:
        map_ref, ft_ref, angle_ref, mine_out, other_out, rt_ref, acc_ref, sem = refs
        mine_in = other_in = None
    else:
        map_ref, ft_ref, angle_ref, mine_in, other_in, mine_out, other_out, rt_ref, acc_ref, sem = refs
    step = pl.program_id(0)
    me = core[0]

    def loads():
        return (
            pltpu.make_async_copy(mine_in, acc_ref.at[me], sem.at[0]),
            pltpu.make_async_copy(other_in, acc_ref.at[1 - me], sem.at[1]),
        )

    if not first:

        @pl.when(step == 0)
        def _():
            for copy in loads():
                copy.start()

    ft = ft_ref[...]
    cols, samples = ft.shape
    lanes = map_ref.shape[1]
    steps = pl.num_programs(0)

    def down(row):
        return jnp.broadcast_to(row, (lanes, lanes)).T

    def arm(k):
        source = down(map_ref[pl.ds(k * steps + step, 1), :].astype(jnp.float32))
        index = lax.broadcasted_iota(jnp.int32, (lanes, lanes), 1).astype(jnp.float32)
        pick = [jnp.where(source - c == index, 1.0, 0.0) for c in range(0, cols, lanes)]
        pick = jnp.concatenate(pick, axis=1).astype(jnp.bfloat16)
        return jnp.dot(pick, ft, preferred_element_type=jnp.float32)

    first_arm, middle_arm, last_arm = (arm(k) for k in range(3))
    shear = 2.0 * middle_arm - first_arm - last_arm
    angle = angle_ref[pl.ds(step, 1), :]
    cosine, sine = jnp.cos(angle), jnp.sin(angle)
    cos_sq, sin_sq, mixed = (
        jnp.tile(down(c), (1, samples // lanes))
        for c in (cosine * cosine, sine * sine, sine * cosine)
    )
    twist = shear * mixed
    along_x = first_arm * cos_sq + last_arm * sin_sq + twist
    along_y = first_arm * sin_sq + last_arm * cos_sq - twist
    shear_new = 2.0 * (last_arm - first_arm) * mixed + shear * (cos_sq - sin_sq)
    per_arm = rt_ref.shape[0] // 3
    here = pl.multiple_of(step * lanes, lanes)
    for k, value in enumerate((along_x, along_y, shear_new)):
        rt_ref[pl.ds(k * per_arm + here, lanes), :] = value.astype(jnp.bfloat16)

    @pl.when(step == pl.num_programs(0) - 1)
    def _():
        if not first:
            for copy in loads():
                copy.wait()
        nb = layout.nb

        def add(idx, block):
            for at, chip, row, n in layout.pieces(idx // CORES):
                here = (idx % CORES, chip, slice(row, row + n))
                if first:
                    acc_ref[here] = block[at : at + n]
                else:
                    acc_ref[here] += block[at : at + n]

        if first:
            for idx in range(layout.used, CORES * layout.half):
                add(idx, jnp.zeros((TILE, TILE), jnp.float32))
        for j in range(0, nb, 2):
            part = dot_nt(rt_ref[0 : TILE * (j + 2), :], rt_ref[TILE * j : TILE * (j + 2), :])
            for i in range(j + 2):
                for jj in range(max(i, j), j + 2):
                    cut = slice(TILE * (jj - j), TILE * (jj - j + 1))
                    add(layout.number[i, jj], part[TILE * i : TILE * (i + 1), cut])
        stores = (
            pltpu.make_async_copy(acc_ref.at[me], mine_out, sem.at[0]),
            pltpu.make_async_copy(acc_ref.at[1 - me], other_out, sem.at[1]),
        )
        for copy in stores:
            copy.start()
        for copy in stores:
            copy.wait()


def gram_chunk(layout, core, arms, ft, angles, so_far):
    cols, samples = ft.shape
    run = (layout.plane, sum(layout.share), TILE)
    shape = jax.ShapeDtypeStruct(run, jnp.float32)
    anywhere = pl.BlockSpec(memory_space=pl.ANY)
    return pl.pallas_call(
        functools.partial(gram_kernel, layout, so_far is None),
        out_shape=(shape, shape),
        grid_spec=pltpu.PrefetchScalarGridSpec(
            num_scalar_prefetch=1,
            grid=(angles.shape[0],),
            in_specs=[
                pl.BlockSpec(arms.shape, lambda g, core: (0, 0)),
                pl.BlockSpec((cols, samples), lambda g, core: (0, 0)),
                pl.BlockSpec(angles.shape, lambda g, core: (0, 0)),
            ]
            + ([] if so_far is None else [anywhere, anywhere]),
            out_specs=(anywhere, anywhere),
            scratch_shapes=[
                pltpu.VMEM((cols, samples), jnp.bfloat16),
                pltpu.VMEM((CORES, *run), jnp.float32),
                pltpu.SemaphoreType.DMA((2,)),
            ],
        ),
        compiler_params=pltpu.CompilerParams(vmem_limit_bytes=VMEM_BYTES),
        name="rotate_gram",
    )(core, arms, ft, angles, *(() if so_far is None else so_far))


def split3(x):
    high = x.astype(jnp.bfloat16).astype(jnp.float32)
    rest = x - high
    middle = rest.astype(jnp.bfloat16).astype(jnp.float32)
    return high, middle, rest - middle


def outer_product(a, b):
    a1, a2, a3 = split3(a)
    b1, b2, b3 = split3(b)
    left = jnp.concatenate([a1, a1, a2, a2, a1, a3], axis=0).astype(jnp.bfloat16)
    right = jnp.concatenate([b1, b2, b1, b2, b3, b1], axis=0).astype(jnp.bfloat16)
    return lax.dot_general(
        left, right, (((0,), (0,)), ((), ())), preferred_element_type=jnp.float32
    )


def factor_block(a_ref, e_ref):
    lane = lax.broadcasted_iota(jnp.int32, (8, TILE), 1)
    sub = lax.broadcasted_iota(jnp.int32, (8, TILE), 0)
    strips = TILE // 8
    work = [a_ref[8 * t : 8 * t + 8, :] for t in range(strips)]

    def columns(x, r0):
        return [jnp.broadcast_to(x[:, r0 + j : r0 + j + 1], (8, TILE)) for j in range(8)]

    def row_of(x, j):
        return jnp.broadcast_to(x[j : j + 1, :], (8, TILE))

    top = columns(work[0], 0)
    for s in range(strips):
        r0 = 8 * s
        below = strips - 1 - s
        here = (lane >= r0) & (lane < r0 + 8)
        cur = jnp.where(here, jnp.where(lane == r0 + sub, 1.0, 0.0), work[s])
        if below:
            low = columns(work[s + 1], r0)
            top2 = columns(work[s], r0 + 8)
            low2 = columns(work[s + 1], r0 + 8)
            nxt = jnp.where(here, 0.0, work[s + 1])
        if below > 1:
            third = columns(work[s + 2], r0)
            nxt2 = jnp.where(here, 0.0, work[s + 2])
        for j in range(8):
            inv = 1.0 / row_of(top[j], j)
            m_top = jnp.where(sub > j, top[j] * inv, 0.0)
            m_low = low[j] * inv if below else None
            m_third = third[j] * inv if below > 1 else None
            for k in range(j + 1, 8):
                c = row_of(top[k], j)
                if k == j + 1:
                    top[k] = top[k] - jnp.where(sub > j, top[j] * c, 0.0) * inv
                else:
                    top[k] = top[k] - m_top * c
                if below:
                    low[k] = low[k] - m_low * c
                if below > 1:
                    third[k] = third[k] - m_third * c
            if below:
                for k in range(8):
                    c = row_of(top2[k], j)
                    if j < 7:
                        top2[k] = top2[k] - m_top * c
                    low2[k] = low2[k] - m_low * c
            row = row_of(cur, j)
            cur = cur - m_top * row
            if below:
                nxt = nxt - m_low * row
            if below > 1:
                nxt2 = nxt2 - m_third * row
        pivot = top[0]
        for j in range(1, 8):
            pivot = jnp.where(sub == j, top[j], pivot)
        scale = lax.rsqrt(pivot)
        cur = cur * scale
        later = jnp.where(lane >= r0 + 8, cur, 0.0)
        out = later
        for k in range(8):
            out = jnp.where((lane == r0 + k) & (sub <= k), top[k] * scale, out)
        a_ref[r0 : r0 + 8, :] = out
        e_ref[r0 : r0 + 8, :] = jnp.where(lane < r0 + 8, cur, 0.0)
        if below:
            work[s + 1] = nxt
            top = low2
        if below > 1:
            work[s + 2] = nxt2
        if below > 2:
            update = outer_product(later, cur)
            for t in range(s + 3, strips):
                work[t] = jnp.where(here, 0.0, work[t]) - update[8 * t : 8 * t + 8, :]


def dot_parts(a, b, contract):
    return lax.dot_general(
        a, b, (((contract,), (0,)), ((), ())), preferred_element_type=jnp.float32
    )


def product(left, right, contract):
    if left[0].shape[contract] <= TILE:
        pairs = ((0, 0), (0, 1), (1, 0), (1, 1), (0, 2), (2, 0))
        return dot_parts(
            jnp.concatenate([left[p] for p, _ in pairs], axis=contract),
            jnp.concatenate([right[q] for _, q in pairs], axis=0),
            contract,
        )
    m = left[0].shape[1 - contract]
    p = dot_parts(jnp.concatenate(left, axis=1 - contract), right[0], contract)
    q = dot_parts(jnp.concatenate(left[:2], axis=1 - contract), right[1], contract)
    r = dot_parts(left[0], right[2], contract)
    return p[:m] + ((p[m : 2 * m] + q[:m]) + ((p[2 * m :] + q[m:]) + r))


def parts3(x):
    return [v.astype(jnp.bfloat16) for v in split3(x)]


def cholesky_kernel(layout, scale, leading, core, *refs):
    n_in = 2 if leading else 6
    sources, refs = refs[:n_in], refs[n_in:]
    out_ref, refs = refs[0], refs[1:]
    if leading:
        inverse_ref, refs = refs[0], refs[1:]
    u_ref, g_ref, a_ref, e_ref, s_ref, p_ref, i_ref, in_sem, out_sem = refs
    me = core[0]
    nb, lead, early = layout.nb, layout.lead, layout.early
    begin, end = (0, lead) if leading else (lead, nb)
    edge = TILE * lead
    size = edge if leading else TILE * nb
    square = (slice(0, edge), slice(0, edge))
    corner = (slice(0, edge), slice(edge, TILE * nb))

    def part_loads(pair, lo, hi, to, sems):
        mine, other = pair
        n = hi - lo
        return [
            pltpu.make_async_copy(mine.at[lo:hi], g_ref.at[me, to : to + n], in_sem.at[sems]),
            pltpu.make_async_copy(
                other.at[lo:hi], g_ref.at[1 - me, to : to + n], in_sem.at[sems + 1]
            ),
        ]

    if leading:
        loads = part_loads(sources[:2], 0, early, 0, 0)
    else:
        first = layout.leading // CORES
        loads = part_loads(sources[2:4], 0, layout.half - early, early, 2)
        if first < early:
            loads += part_loads(sources[:2], first, early, first, 0)
        loads.append(pltpu.make_async_copy(sources[4].at[square], u_ref.at[square], in_sem.at[4]))
        loads.append(pltpu.make_async_copy(sources[5], i_ref, in_sem.at[5]))

    def store(k):
        here = (slice(TILE * k, TILE * (k + 1)), slice(0, size))
        return pltpu.make_async_copy(u_ref.at[here], out_ref.at[here], out_sem.at[k])

    def gram(i, j):
        n = layout.number[i, j]
        return g_ref[n % CORES, n // CORES] * scale

    def up(rows, cols):
        return [p_ref[q, rows, cols] for q in range(3)]

    def keep(rows, cols, value):
        for q, v in enumerate(parts3(value)):
            p_ref[q, rows, cols] = v

    for copy in loads:
        copy.start()
    for copy in loads:
        copy.wait()

    stores = []
    if not leading:
        right = slice(edge, size)
        for k in range(lead):
            rows, cols = slice(TILE * k, TILE * (k + 1)), slice(TILE * k, edge)
            keep(rows, cols, u_ref[rows, cols])
        for k in range(lead):
            rows = slice(TILE * k, TILE * (k + 1))
            above = slice(0, TILE * k)
            value = jnp.concatenate([gram(k, j) for j in range(lead, nb)], axis=1)
            if k:
                value = value - product(up(above, rows), up(above, right), 0)
            value = product(parts3(i_ref[k]), parts3(value), 1)
            u_ref[rows, right] = value
            keep(rows, right, value)
        stores.append(
            pltpu.make_async_copy(u_ref.at[corner], out_ref.at[corner], out_sem.at[0])
        )
        stores[0].start()

    def body(i, carry):
        for k in range(begin, end):
            h = k % 2
            r0 = TILE * (k - h)
            c0 = TILE * k

            @pl.when(i == k)
            def _(k=k, h=h, r0=r0, c0=c0):
                if h == 0:
                    for hh in range(2):
                        for j in range(k, size // TILE):
                            if j < k + hh:
                                block = jnp.zeros((TILE, TILE), jnp.float32)
                            else:
                                block = gram(k + hh, j)
                            s_ref[TILE * hh : TILE * (hh + 1), TILE * j : TILE * (j + 1)] = block
                    if r0:
                        panel = slice(r0, r0 + 2 * TILE)
                        s_ref[:, r0:size] -= product(
                            up(slice(0, r0), panel), up(slice(0, r0), slice(r0, size)), 0
                        )
                else:
                    above = slice(r0, c0)
                    s_ref[TILE:, c0:size] -= product(
                        up(above, slice(c0, c0 + TILE)), up(above, slice(c0, size)), 0
                    )
                a_ref[...] = s_ref[TILE * h : TILE * (h + 1), c0 : c0 + TILE]

        factor_block(a_ref, e_ref)
        for k in range(begin, end):
            h = k % 2
            c0 = TILE * k

            @pl.when(i == k)
            def _(k=k, h=h, c0=c0):
                rows = slice(c0, c0 + TILE)
                if c0:
                    u_ref[rows, 0:c0] = jnp.zeros((TILE, c0), jnp.float32)
                u_ref[rows, c0 : c0 + TILE] = a_ref[...]
                if leading:
                    i_ref[k] = e_ref[...]
                if c0 + TILE < size:
                    rest = slice(c0 + TILE, size)
                    solved = product(
                        parts3(e_ref[...]), parts3(s_ref[TILE * h : TILE * (h + 1), rest]), 1
                    )
                    u_ref[rows, rest] = solved
                    keep(rows, rest, solved)
                store(k).start()

        return carry

    lax.fori_loop(begin, end, body, 0)
    if leading:
        stores.append(pltpu.make_async_copy(i_ref, inverse_ref, in_sem.at[4]))
        stores[0].start()
    stores += [store(k) for k in range(begin, end)]
    for copy in stores:
        copy.wait()


def cholesky_part(layout, core, groups, so_far, scale):
    size = layout.nb * TILE
    leading = so_far is None
    anywhere = pl.BlockSpec(memory_space=pl.ANY)
    sources = [x for pair in groups for x in pair] + ([] if leading else list(so_far))
    factor = jax.ShapeDtypeStruct((size, size), jnp.float32)
    inverses = jax.ShapeDtypeStruct((layout.lead, TILE, TILE), jnp.float32)
    blocks = layout.lead if leading else layout.nb - layout.lead
    return pl.pallas_call(
        functools.partial(cholesky_kernel, layout, scale, leading),
        out_shape=(factor, inverses) if leading else factor,
        grid_spec=pltpu.PrefetchScalarGridSpec(
            num_scalar_prefetch=1,
            grid=(1,),
            in_specs=[anywhere] * len(sources),
            out_specs=(anywhere, anywhere) if leading else anywhere,
            scratch_shapes=[
                pltpu.VMEM((size, size), jnp.float32),
                pltpu.VMEM((CORES, layout.half, TILE, TILE), jnp.float32),
                pltpu.VMEM((TILE, TILE), jnp.float32),
                pltpu.VMEM((TILE, TILE), jnp.float32),
                pltpu.VMEM((2 * TILE, size), jnp.float32),
                pltpu.VMEM((3, size, size), jnp.bfloat16),
                pltpu.VMEM((layout.lead, TILE, TILE), jnp.float32),
                pltpu.SemaphoreType.DMA((6,)),
                pltpu.SemaphoreType.DMA((layout.nb,)),
            ],
        ),
        input_output_aliases={} if leading else {len(sources) - 1: 0},
        cost_estimate=pl.CostEstimate(
            flops=40 * blocks * size**2 * TILE, transcendentals=0, bytes_accessed=12 * size**2
        ),
        compiler_params=pltpu.CompilerParams(vmem_limit_bytes=VMEM_BYTES),
        name="cholesky",
    )(core, *sources)


def swap_cores(x):
    return lax.ppermute(x, "core", [(0, 1), (1, 0)])


def gather_plane(copies):
    return lax.all_to_all(copies, PLANE_AXES, split_axis=0, concat_axis=0, tiled=True)


def shards(records, offsets, column_map, angles):
    parts = lax.axis_size(GAUGE_AXES)
    rows, cols_here = records.shape
    cols = column_map.shape[0]
    core = lax.axis_index("core").astype(jnp.int32).reshape(1)
    records_t = records.T
    arms = column_map.reshape(-1, TILE)
    angles = angles.reshape(-1, TILE)
    layout = Layout(cols // TILE, lax.axis_size(PLANE_AXES))
    acc = None
    for filtered in filter_records(records_t, offsets, parts):
        regrouped = lax.all_to_all(filtered, GAUGE_AXES, split_axis=0, concat_axis=0, tiled=True)
        acc = gram_chunk(layout, core, arms, regrouped.reshape(cols, -1), angles, acc)
    mine, other = acc
    mine = mine + swap_cores(other)
    spread = lax.all_to_all(mine, PLANE_AXES, split_axis=0, concat_axis=0, tiled=True).sum(0)
    scale = 1.0 / (rows * lax.axis_size(SAMPLE_AXES))
    early, late = (
        jnp.broadcast_to(x[None], (layout.plane, *x.shape))
        for x in jnp.split(spread, [layout.share[0]])
    )
    early = gather_plane(early)
    late, early = lax.optimization_barrier((late, early))
    late = gather_plane(late)
    early, late = (g.reshape(-1, TILE, TILE) for g in (early, late))
    groups = [(early, swap_cores(early))]
    upper, inverses = cholesky_part(layout, core, groups, None, scale)
    late, upper = lax.optimization_barrier((late, upper))
    groups.append((late, swap_cores(late)))
    return cholesky_part(layout, core, groups, (upper, inverses), scale)


def solution(mesh):
    devices = mesh.devices
    tm, gauge = devices.shape
    side = int(round(tm**0.5))
    fine = Mesh(
        devices.reshape(side, tm // side, gauge // CORES, CORES), SAMPLE_AXES + GAUGE_AXES
    )
    placed = (P(SAMPLE_AXES, GAUGE_AXES), P(SAMPLE_AXES), P(), P())
    return jax.shard_map(shards, mesh=fine, in_specs=placed, out_specs=P(), check_vma=False)
```

```python
import functools

import jax
import jax.numpy as jnp
from jax import lax
from jax.experimental import pallas as pl
from jax.experimental.pallas import tpu as pltpu
from jax.sharding import Mesh
from jax.sharding import PartitionSpec as P

BLOCK = 1024
BAND = 64
TILE = 128
CORES = 2
SAMPLE_AXES = ("z", "x")
GAUGE_AXES = ("y", "core")
PLANE_AXES = ("z", "x", "y")
HIGHEST = lax.Precision.HIGHEST
VMEM_BYTES = 54 * 1024 * 1024
GRAM_BYTES = 50 * 1024 * 1024


class Layout:
    def __init__(self, nb, plane):
        self.nb, self.plane = nb, plane
        self.lead = lead = nb // 4 * 2
        order = [(i, j) for i in range(lead) for j in range(i, lead)]
        self.leading = len(order)
        order += [(i, j) for i in range(nb) for j in range(max(i, lead), nb)]
        self.number = {ij: n for n, ij in enumerate(order)}
        self.used = len(order)
        step = max(1, 8 * plane // TILE)
        self.early = -(-(-(-self.leading // CORES)) // step) * step
        self.half = -(-(-(-self.used // CORES)) // step) * step
        self.share = (self.early * TILE // plane, (self.half - self.early) * TILE // plane)

    def pieces(self, position):
        late = position >= self.early
        share = self.share[late]
        base = self.share[0] if late else 0
        row = (position - (self.early if late else 0)) * TILE
        at, out = 0, []
        while at < TILE:
            chip, inside = divmod(row + at, share)
            n = min(share - inside, TILE - at)
            out.append((at, chip, base + inside, n))
            at += n
        return out


def dot_nt(a, b):
    return lax.dot_general(a, b, (((1,), (1,)), ((), ())), preferred_element_type=jnp.float32)


def filter_kernel(offsets, x_ref, head_ref, tail_ref):
    parts, _, split = head_ref.shape
    blocks = x_ref.shape[1] // BLOCK // parts
    for b in range(parts * blocks):
        start = offsets[pl.program_id(0) * parts * blocks + b]
        x = x_ref[:, b * BLOCK : (b + 1) * BLOCK]
        sample = lax.broadcasted_iota(jnp.int32, (1, BLOCK), 1)
        inside = jnp.where((sample >= start) & (sample < start + BAND), 1.0, 0.0)
        mask = jnp.broadcast_to(inside.astype(jnp.bfloat16), (TILE, BLOCK))
        baseline = dot_nt(x, mask) * (1.0 / BAND)
        for t in range(0, BLOCK, TILE):
            value = (x[:, t : t + TILE].astype(jnp.float32) - baseline).astype(jnp.bfloat16)
            here = b % blocks * BLOCK + t
            if here < split:
                head_ref[b // blocks, :, here : here + TILE] = value
            else:
                tail_ref[b // blocks, :, here - split : here - split + TILE] = value


def filter_records(records_t, offsets, parts):
    rows, samples = records_t.shape
    each = samples // parts
    tail = BLOCK // 2
    widths = (each - tail, tail)
    per = 2
    return pl.pallas_call(
        filter_kernel,
        out_shape=tuple(jax.ShapeDtypeStruct((parts, rows, w), jnp.bfloat16) for w in widths),
        grid_spec=pltpu.PrefetchScalarGridSpec(
            num_scalar_prefetch=1,
            grid=(parts // per,),
            in_specs=[pl.BlockSpec((rows, per * each), lambda d, off: (0, d))],
            out_specs=tuple(
                pl.BlockSpec((per, rows, w), lambda d, off: (d, 0, 0)) for w in widths
            ),
        ),
        compiler_params=pltpu.CompilerParams(vmem_limit_bytes=VMEM_BYTES),
        name="drift_filter",
    )(offsets, records_t)


def gram_kernel(layout, first, core, *refs):
    if first:
        map_ref, ft_ref, angle_ref, mine_out, other_out, rt_ref, acc_ref, sem = refs
        mine_in = other_in = None
    else:
        map_ref, ft_ref, angle_ref, mine_in, other_in, mine_out, other_out, rt_ref, acc_ref, sem = refs
    step = pl.program_id(0)
    me = core[0]

    def loads():
        return (
            pltpu.make_async_copy(mine_in, acc_ref.at[me], sem.at[0]),
            pltpu.make_async_copy(other_in, acc_ref.at[1 - me], sem.at[1]),
        )

    if not first:

        @pl.when(step == 0)
        def _():
            for copy in loads():
                copy.start()

    ft = ft_ref[...]
    cols, samples = ft.shape
    lanes = map_ref.shape[1]
    steps = pl.num_programs(0)

    def down(row):
        return jnp.broadcast_to(row, (lanes, lanes)).T

    def arm(k):
        source = down(map_ref[pl.ds(k * steps + step, 1), :].astype(jnp.float32))
        index = lax.broadcasted_iota(jnp.int32, (lanes, lanes), 1).astype(jnp.float32)
        pick = [jnp.where(source - c == index, 1.0, 0.0) for c in range(0, cols, lanes)]
        pick = jnp.concatenate(pick, axis=1).astype(jnp.bfloat16)
        return jnp.dot(pick, ft, preferred_element_type=jnp.float32)

    first_arm, middle_arm, last_arm = (arm(k) for k in range(3))
    shear = 2.0 * middle_arm - first_arm - last_arm
    angle = angle_ref[pl.ds(step, 1), :]
    cosine, sine = jnp.cos(angle), jnp.sin(angle)
    cos_sq, sin_sq, mixed = (
        jnp.tile(down(c), (1, samples // lanes))
        for c in (cosine * cosine, sine * sine, sine * cosine)
    )
    twist = shear * mixed
    along_x = first_arm * cos_sq + last_arm * sin_sq + twist
    along_y = first_arm * sin_sq + last_arm * cos_sq - twist
    shear_new = 2.0 * (last_arm - first_arm) * mixed + shear * (cos_sq - sin_sq)
    per_arm = rt_ref.shape[0] // 3
    here = pl.multiple_of(step * lanes, lanes)
    for k, value in enumerate((along_x, along_y, shear_new)):
        rt_ref[pl.ds(k * per_arm + here, lanes), :] = value.astype(jnp.bfloat16)

    @pl.when(step == pl.num_programs(0) - 1)
    def _():
        if not first:
            for copy in loads():
                copy.wait()
        nb = layout.nb

        def add(idx, block):
            for at, chip, row, n in layout.pieces(idx // CORES):
                here = (idx % CORES, chip, slice(row, row + n))
                if first:
                    acc_ref[here] = block[at : at + n]
                else:
                    acc_ref[here] += block[at : at + n]

        if first:
            for idx in range(layout.used, CORES * layout.half):
                add(idx, jnp.zeros((TILE, TILE), jnp.float32))
        for j in range(0, nb, 2):
            part = dot_nt(rt_ref[0 : TILE * (j + 2), :], rt_ref[TILE * j : TILE * (j + 2), :])
            for i in range(j + 2):
                for jj in range(max(i, j), j + 2):
                    cut = slice(TILE * (jj - j), TILE * (jj - j + 1))
                    add(layout.number[i, jj], part[TILE * i : TILE * (i + 1), cut])
        stores = (
            pltpu.make_async_copy(acc_ref.at[me], mine_out, sem.at[0]),
            pltpu.make_async_copy(acc_ref.at[1 - me], other_out, sem.at[1]),
        )
        for copy in stores:
            copy.start()
        for copy in stores:
            copy.wait()


def gram_chunk(layout, core, arms, ft, angles, so_far):
    cols, samples = ft.shape
    run = (layout.plane, sum(layout.share), TILE)
    anywhere = pl.BlockSpec(memory_space=pl.ANY)
    if so_far is None:
        shape, place = jax.ShapeDtypeStruct(run, jnp.float32), anywhere
    else:
        shape, place = pltpu.VMEM(run, jnp.float32), pl.BlockSpec(memory_space=pltpu.VMEM)
    return pl.pallas_call(
        functools.partial(gram_kernel, layout, so_far is None),
        out_shape=(shape, shape),
        grid_spec=pltpu.PrefetchScalarGridSpec(
            num_scalar_prefetch=1,
            grid=(angles.shape[0],),
            in_specs=[
                pl.BlockSpec(arms.shape, lambda g, core: (0, 0)),
                pl.BlockSpec((cols, samples), lambda g, core: (0, 0))
                if so_far is None
                else pl.BlockSpec(memory_space=pltpu.VMEM),
                pl.BlockSpec(angles.shape, lambda g, core: (0, 0)),
            ]
            + ([] if so_far is None else [anywhere, anywhere]),
            out_specs=(place, place),
            scratch_shapes=[
                pltpu.VMEM((cols, samples), jnp.bfloat16),
                pltpu.VMEM((CORES, *run), jnp.float32),
                pltpu.SemaphoreType.DMA((2,)),
            ],
        ),
        compiler_params=pltpu.CompilerParams(vmem_limit_bytes=VMEM_BYTES if so_far is None else GRAM_BYTES),
        name="rotate_gram",
    )(core, arms, ft if so_far is None else pltpu.with_memory_space_constraint(ft, pltpu.VMEM), angles, *(() if so_far is None else so_far))


def split3(x):
    high = x.astype(jnp.bfloat16).astype(jnp.float32)
    rest = x - high
    middle = rest.astype(jnp.bfloat16).astype(jnp.float32)
    return high, middle, rest - middle


def outer_product(a, b):
    a1, a2, a3 = split3(a)
    b1, b2, b3 = split3(b)
    left = jnp.concatenate([a1, a1, a2, a2, a1, a3], axis=0).astype(jnp.bfloat16)
    right = jnp.concatenate([b1, b2, b1, b2, b3, b1], axis=0).astype(jnp.bfloat16)
    return lax.dot_general(
        left, right, (((0,), (0,)), ((), ())), preferred_element_type=jnp.float32
    )


def factor_block(a_ref, e_ref):
    lane = lax.broadcasted_iota(jnp.int32, (8, TILE), 1)
    sub = lax.broadcasted_iota(jnp.int32, (8, TILE), 0)
    strips = TILE // 8
    work = [a_ref[8 * t : 8 * t + 8, :] for t in range(strips)]

    def columns(x, r0):
        return [jnp.broadcast_to(x[:, r0 + j : r0 + j + 1], (8, TILE)) for j in range(8)]

    def row_of(x, j):
        return jnp.broadcast_to(x[j : j + 1, :], (8, TILE))

    top = columns(work[0], 0)
    for s in range(strips):
        r0 = 8 * s
        below = strips - 1 - s
        here = (lane >= r0) & (lane < r0 + 8)
        cur = jnp.where(here, jnp.where(lane == r0 + sub, 1.0, 0.0), work[s])
        if below:
            low = columns(work[s + 1], r0)
            top2 = columns(work[s], r0 + 8)
            low2 = columns(work[s + 1], r0 + 8)
            nxt = jnp.where(here, 0.0, work[s + 1])
        if below > 1:
            third = columns(work[s + 2], r0)
            nxt2 = jnp.where(here, 0.0, work[s + 2])
        for j in range(8):
            inv = 1.0 / row_of(top[j], j)
            m_top = jnp.where(sub > j, top[j] * inv, 0.0)
            m_low = low[j] * inv if below else None
            m_third = third[j] * inv if below > 1 else None
            for k in range(j + 1, 8):
                c = row_of(top[k], j)
                if k == j + 1:
                    top[k] = top[k] - jnp.where(sub > j, top[j] * c, 0.0) * inv
                else:
                    top[k] = top[k] - m_top * c
                if below:
                    low[k] = low[k] - m_low * c
                if below > 1:
                    third[k] = third[k] - m_third * c
            if below:
                for k in range(8):
                    c = row_of(top2[k], j)
                    if j < 7:
                        top2[k] = top2[k] - m_top * c
                    low2[k] = low2[k] - m_low * c
            row = row_of(cur, j)
            cur = cur - m_top * row
            if below:
                nxt = nxt - m_low * row
            if below > 1:
                nxt2 = nxt2 - m_third * row
        pivot = top[0]
        for j in range(1, 8):
            pivot = jnp.where(sub == j, top[j], pivot)
        scale = lax.rsqrt(pivot)
        cur = cur * scale
        later = jnp.where(lane >= r0 + 8, cur, 0.0)
        out = later
        for k in range(8):
            out = jnp.where((lane == r0 + k) & (sub <= k), top[k] * scale, out)
        a_ref[r0 : r0 + 8, :] = out
        e_ref[r0 : r0 + 8, :] = jnp.where(lane < r0 + 8, cur, 0.0)
        if below:
            work[s + 1] = nxt
            top = low2
        if below > 1:
            work[s + 2] = nxt2
        if below > 2:
            update = outer_product(later, cur)
            for t in range(s + 3, strips):
                work[t] = jnp.where(here, 0.0, work[t]) - update[8 * t : 8 * t + 8, :]


def dot_parts(a, b, contract):
    return lax.dot_general(
        a, b, (((contract,), (0,)), ((), ())), preferred_element_type=jnp.float32
    )


def product(left, right, contract):
    if left[0].shape[contract] <= TILE:
        pairs = ((0, 0), (0, 1), (1, 0), (1, 1), (0, 2), (2, 0))
        return dot_parts(
            jnp.concatenate([left[p] for p, _ in pairs], axis=contract),
            jnp.concatenate([right[q] for _, q in pairs], axis=0),
            contract,
        )
    m = left[0].shape[1 - contract]
    p = dot_parts(jnp.concatenate(left, axis=1 - contract), right[0], contract)
    q = dot_parts(jnp.concatenate(left[:2], axis=1 - contract), right[1], contract)
    r = dot_parts(left[0], right[2], contract)
    return p[:m] + ((p[m : 2 * m] + q[:m]) + ((p[2 * m :] + q[m:]) + r))


def parts3(x):
    return [v.astype(jnp.bfloat16) for v in split3(x)]


def cholesky_kernel(layout, scale, leading, core, *refs):
    n_in = 2 if leading else 6
    sources, refs = refs[:n_in], refs[n_in:]
    out_ref, refs = refs[0], refs[1:]
    if leading:
        inverse_ref, refs = refs[0], refs[1:]
    u_ref, g_ref, a_ref, e_ref, s_ref, p_ref, i_ref, in_sem, out_sem = refs
    me = core[0]
    nb, lead, early = layout.nb, layout.lead, layout.early
    begin, end = (0, lead) if leading else (lead, nb)
    edge = TILE * lead
    size = edge if leading else TILE * nb
    square = (slice(0, edge), slice(0, edge))
    corner = (slice(0, edge), slice(edge, TILE * nb))

    def part_loads(pair, lo, hi, to, sems):
        mine, other = pair
        n = hi - lo
        return [
            pltpu.make_async_copy(mine.at[lo:hi], g_ref.at[me, to : to + n], in_sem.at[sems]),
            pltpu.make_async_copy(
                other.at[lo:hi], g_ref.at[1 - me, to : to + n], in_sem.at[sems + 1]
            ),
        ]

    if leading:
        loads = part_loads(sources[:2], 0, early, 0, 0)
    else:
        first = layout.leading // CORES
        loads = part_loads(sources[2:4], 0, layout.half - early, early, 2)
        if first < early:
            loads += part_loads(sources[:2], first, early, first, 0)
        loads.append(pltpu.make_async_copy(sources[4].at[square], u_ref.at[square], in_sem.at[4]))
        loads.append(pltpu.make_async_copy(sources[5], i_ref, in_sem.at[5]))

    def store(k):
        here = (slice(TILE * k, TILE * (k + 1)), slice(0, size))
        return pltpu.make_async_copy(u_ref.at[here], out_ref.at[here], out_sem.at[k])

    def gram(i, j):
        n = layout.number[i, j]
        return g_ref[n % CORES, n // CORES] * scale

    def up(rows, cols):
        return [p_ref[q, rows, cols] for q in range(3)]

    def keep(rows, cols, value):
        for q, v in enumerate(parts3(value)):
            p_ref[q, rows, cols] = v

    for copy in loads:
        copy.start()
    for copy in loads:
        copy.wait()

    stores = []
    if not leading:
        right = slice(edge, size)
        for k in range(lead):
            rows, cols = slice(TILE * k, TILE * (k + 1)), slice(TILE * k, edge)
            keep(rows, cols, u_ref[rows, cols])
        for k in range(lead):
            rows = slice(TILE * k, TILE * (k + 1))
            above = slice(0, TILE * k)
            value = jnp.concatenate([gram(k, j) for j in range(lead, nb)], axis=1)
            if k:
                value = value - product(up(above, rows), up(above, right), 0)
            value = product(parts3(i_ref[k]), parts3(value), 1)
            u_ref[rows, right] = value
            keep(rows, right, value)
        stores.append(
            pltpu.make_async_copy(u_ref.at[corner], out_ref.at[corner], out_sem.at[0])
        )
        stores[0].start()

    def body(i, carry):
        for k in range(begin, end):
            h = k % 2
            r0 = TILE * (k - h)
            c0 = TILE * k

            @pl.when(i == k)
            def _(k=k, h=h, r0=r0, c0=c0):
                if h == 0:
                    for hh in range(2):
                        for j in range(k, size // TILE):
                            if j < k + hh:
                                block = jnp.zeros((TILE, TILE), jnp.float32)
                            else:
                                block = gram(k + hh, j)
                            s_ref[TILE * hh : TILE * (hh + 1), TILE * j : TILE * (j + 1)] = block
                    if r0:
                        panel = slice(r0, r0 + 2 * TILE)
                        s_ref[:, r0:size] -= product(
                            up(slice(0, r0), panel), up(slice(0, r0), slice(r0, size)), 0
                        )
                else:
                    above = slice(r0, c0)
                    s_ref[TILE:, c0:size] -= product(
                        up(above, slice(c0, c0 + TILE)), up(above, slice(c0, size)), 0
                    )
                a_ref[...] = s_ref[TILE * h : TILE * (h + 1), c0 : c0 + TILE]

        factor_block(a_ref, e_ref)
        for k in range(begin, end):
            h = k % 2
            c0 = TILE * k

            @pl.when(i == k)
            def _(k=k, h=h, c0=c0):
                rows = slice(c0, c0 + TILE)
                if c0:
                    u_ref[rows, 0:c0] = jnp.zeros((TILE, c0), jnp.float32)
                u_ref[rows, c0 : c0 + TILE] = a_ref[...]
                if leading:
                    i_ref[k] = e_ref[...]
                if c0 + TILE < size:
                    rest = slice(c0 + TILE, size)
                    solved = product(
                        parts3(e_ref[...]), parts3(s_ref[TILE * h : TILE * (h + 1), rest]), 1
                    )
                    u_ref[rows, rest] = solved
                    keep(rows, rest, solved)
                store(k).start()

        return carry

    lax.fori_loop(begin, end, body, 0)
    if leading:
        stores.append(pltpu.make_async_copy(i_ref, inverse_ref, in_sem.at[4]))
        stores[0].start()
    stores += [store(k) for k in range(begin, end)]
    for copy in stores:
        copy.wait()


def cholesky_part(layout, core, groups, so_far, scale):
    size = layout.nb * TILE
    leading = so_far is None
    anywhere = pl.BlockSpec(memory_space=pl.ANY)
    sources = [pltpu.with_memory_space_constraint(x, pltpu.VMEM) for pair in groups for x in pair]
    n_blocks = len(sources)
    sources += [] if leading else list(so_far)
    factor = jax.ShapeDtypeStruct((size, size), jnp.float32)
    inverses = jax.ShapeDtypeStruct((layout.lead, TILE, TILE), jnp.float32)
    blocks = layout.lead if leading else layout.nb - layout.lead
    return pl.pallas_call(
        functools.partial(cholesky_kernel, layout, scale, leading),
        out_shape=(factor, inverses) if leading else factor,
        grid_spec=pltpu.PrefetchScalarGridSpec(
            num_scalar_prefetch=1,
            grid=(1,),
            in_specs=[pl.BlockSpec(memory_space=pltpu.VMEM)] * n_blocks
            + [anywhere] * (len(sources) - n_blocks),
            out_specs=(anywhere, anywhere) if leading else anywhere,
            scratch_shapes=[
                pltpu.VMEM((size, size), jnp.float32),
                pltpu.VMEM((CORES, layout.half, TILE, TILE), jnp.float32),
                pltpu.VMEM((TILE, TILE), jnp.float32),
                pltpu.VMEM((TILE, TILE), jnp.float32),
                pltpu.VMEM((2 * TILE, size), jnp.float32),
                pltpu.VMEM((3, size, size), jnp.bfloat16),
                pltpu.VMEM((layout.lead, TILE, TILE), jnp.float32),
                pltpu.SemaphoreType.DMA((6,)),
                pltpu.SemaphoreType.DMA((layout.nb,)),
            ],
        ),
        input_output_aliases={} if leading else {len(sources) - 1: 0},
        cost_estimate=pl.CostEstimate(
            flops=40 * blocks * size**2 * TILE, transcendentals=0, bytes_accessed=12 * size**2
        ),
        compiler_params=pltpu.CompilerParams(vmem_limit_bytes=VMEM_BYTES),
        name="cholesky",
    )(core, *sources)


def swap_cores(x):
    return lax.ppermute(x, "core", [(0, 1), (1, 0)])


def gather_plane(copies):
    return lax.all_to_all(copies, PLANE_AXES, split_axis=0, concat_axis=0, tiled=True)


def shards(records, offsets, column_map, angles):
    parts = lax.axis_size(GAUGE_AXES)
    rows, cols_here = records.shape
    cols = column_map.shape[0]
    core = lax.axis_index("core").astype(jnp.int32).reshape(1)
    records_t = records.T
    arms = column_map.reshape(-1, TILE)
    angles = angles.reshape(-1, TILE)
    layout = Layout(cols // TILE, lax.axis_size(PLANE_AXES))
    acc = None
    for filtered in filter_records(records_t, offsets, parts):
        regrouped = lax.all_to_all(filtered, GAUGE_AXES, split_axis=0, concat_axis=0, tiled=True)
        acc = gram_chunk(layout, core, arms, regrouped.reshape(cols, -1), angles, acc)
    mine, other = acc
    mine = mine + swap_cores(other)
    spread = lax.all_to_all(mine, PLANE_AXES, split_axis=0, concat_axis=0, tiled=True).sum(0)
    scale = 1.0 / (rows * lax.axis_size(SAMPLE_AXES))
    early, late = (
        jnp.broadcast_to(x[None], (layout.plane, *x.shape))
        for x in jnp.split(spread, [layout.share[0]])
    )
    early = gather_plane(early)
    late, early = lax.optimization_barrier((late, early))
    late = gather_plane(late)
    early, late = (g.reshape(-1, TILE, TILE) for g in (early, late))
    groups = [(early, swap_cores(early))]
    upper, inverses = cholesky_part(layout, core, groups, None, scale)
    late, upper = lax.optimization_barrier((late, upper))
    groups.append((late, swap_cores(late)))
    return cholesky_part(layout, core, groups, (upper, inverses), scale)


def solution(mesh):
    devices = mesh.devices
    tm, gauge = devices.shape
    side = int(round(tm**0.5))
    fine = Mesh(
        devices.reshape(side, tm // side, gauge // CORES, CORES), SAMPLE_AXES + GAUGE_AXES
    )
    placed = (P(SAMPLE_AXES, GAUGE_AXES), P(SAMPLE_AXES), P(), P())
    return jax.shard_map(shards, mesh=fine, in_specs=placed, out_specs=P(), check_vma=False)
```

```python
import functools

import jax
import jax.numpy as jnp
from jax import lax
from jax.experimental import pallas as pl
from jax.experimental.pallas import tpu as pltpu
from jax.sharding import Mesh
from jax.sharding import PartitionSpec as P

BLOCK = 1024
BAND = 64
TILE = 128
CORES = 2
SAMPLE_AXES = ("z", "x")
GAUGE_AXES = ("y", "core")
PLANE_AXES = ("z", "x", "y")
HIGHEST = lax.Precision.HIGHEST
VMEM_BYTES = 54 * 1024 * 1024
GRAM_BYTES = 50 * 1024 * 1024
FILTER_BYTES = 54 * 1024 * 1024
STEPS = 4


class Layout:
    def __init__(self, nb, plane):
        self.nb, self.plane = nb, plane
        self.lead = lead = nb // 4 * 2
        order = [(i, j) for i in range(lead) for j in range(i, lead)]
        self.leading = len(order)
        order += [(i, j) for i in range(nb) for j in range(max(i, lead), nb)]
        self.number = {ij: n for n, ij in enumerate(order)}
        self.used = len(order)
        step = max(1, 8 * plane // TILE)
        self.early = -(-(-(-self.leading // CORES)) // step) * step
        self.half = -(-(-(-self.used // CORES)) // step) * step
        self.share = (self.early * TILE // plane, (self.half - self.early) * TILE // plane)

    def pieces(self, position):
        late = position >= self.early
        share = self.share[late]
        base = self.share[0] if late else 0
        row = (position - (self.early if late else 0)) * TILE
        at, out = 0, []
        while at < TILE:
            chip, inside = divmod(row + at, share)
            n = min(share - inside, TILE - at)
            out.append((at, chip, base + inside, n))
            at += n
        return out


def dot_nt(a, b):
    return lax.dot_general(a, b, (((1,), (1,)), ((), ())), preferred_element_type=jnp.float32)


def filter_kernel(offsets, x_ref, head_ref, tail_ref):
    parts, split = tail_ref.shape[0], head_ref.shape[2]
    step = pl.program_id(0)
    blocks = x_ref.shape[1] // BLOCK // parts
    for b in range(parts * blocks):
        start = offsets[step * parts * blocks + b]
        x = x_ref[:, b * BLOCK : (b + 1) * BLOCK]
        sample = lax.broadcasted_iota(jnp.int32, (1, BLOCK), 1)
        inside = jnp.where((sample >= start) & (sample < start + BAND), 1.0, 0.0)
        mask = jnp.broadcast_to(inside.astype(jnp.bfloat16), (TILE, BLOCK))
        baseline = dot_nt(x, mask) * (1.0 / BAND)
        for t in range(0, BLOCK, TILE):
            value = (x[:, t : t + TILE].astype(jnp.float32) - baseline).astype(jnp.bfloat16)
            here = b % blocks * BLOCK + t
            if here < split:
                head_ref[step * parts + b // blocks, :, here : here + TILE] = value
            else:
                tail_ref[b // blocks, :, here - split : here - split + TILE] = value


def filter_records(records_t, offsets, parts):
    rows, samples = records_t.shape
    each = samples // parts
    tail = BLOCK // 2
    return pl.pallas_call(
        filter_kernel,
        out_shape=(
            pltpu.VMEM((parts, rows, each - tail), jnp.bfloat16),
            jax.ShapeDtypeStruct((parts, rows, tail), jnp.bfloat16),
        ),
        grid_spec=pltpu.PrefetchScalarGridSpec(
            num_scalar_prefetch=1,
            grid=(STEPS,),
            in_specs=[pl.BlockSpec((rows, samples // STEPS), lambda d, off: (0, d))],
            out_specs=(
                pl.BlockSpec(memory_space=pltpu.VMEM),
                pl.BlockSpec((parts // STEPS, rows, tail), lambda d, off: (d, 0, 0)),
            ),
        ),
        compiler_params=pltpu.CompilerParams(vmem_limit_bytes=FILTER_BYTES),
        name="drift_filter",
    )(offsets, records_t)


def gram_kernel(layout, first, core, *refs):
    if first:
        map_ref, ft_ref, angle_ref, mine_out, other_out, rt_ref, acc_ref, sem = refs
        mine_in = other_in = None
    else:
        map_ref, ft_ref, angle_ref, mine_in, other_in, mine_out, other_out, rt_ref, acc_ref, sem = refs
    step = pl.program_id(0)
    me = core[0]

    def loads():
        return (
            pltpu.make_async_copy(mine_in, acc_ref.at[me], sem.at[0]),
            pltpu.make_async_copy(other_in, acc_ref.at[1 - me], sem.at[1]),
        )

    if not first:

        @pl.when(step == 0)
        def _():
            for copy in loads():
                copy.start()

    ft = ft_ref[...]
    cols, samples = ft.shape
    lanes = map_ref.shape[1]
    steps = pl.num_programs(0)

    def down(row):
        return jnp.broadcast_to(row, (lanes, lanes)).T

    def arm(k):
        source = down(map_ref[pl.ds(k * steps + step, 1), :].astype(jnp.float32))
        index = lax.broadcasted_iota(jnp.int32, (lanes, lanes), 1).astype(jnp.float32)
        pick = [jnp.where(source - c == index, 1.0, 0.0) for c in range(0, cols, lanes)]
        pick = jnp.concatenate(pick, axis=1).astype(jnp.bfloat16)
        return jnp.dot(pick, ft, preferred_element_type=jnp.float32)

    first_arm, middle_arm, last_arm = (arm(k) for k in range(3))
    shear = 2.0 * middle_arm - first_arm - last_arm
    angle = angle_ref[pl.ds(step, 1), :]
    cosine, sine = jnp.cos(angle), jnp.sin(angle)
    cos_sq, sin_sq, mixed = (
        jnp.tile(down(c), (1, samples // lanes))
        for c in (cosine * cosine, sine * sine, sine * cosine)
    )
    twist = shear * mixed
    along_x = first_arm * cos_sq + last_arm * sin_sq + twist
    along_y = first_arm * sin_sq + last_arm * cos_sq - twist
    shear_new = 2.0 * (last_arm - first_arm) * mixed + shear * (cos_sq - sin_sq)
    per_arm = rt_ref.shape[0] // 3
    here = pl.multiple_of(step * lanes, lanes)
    for k, value in enumerate((along_x, along_y, shear_new)):
        rt_ref[pl.ds(k * per_arm + here, lanes), :] = value.astype(jnp.bfloat16)

    @pl.when(step == pl.num_programs(0) - 1)
    def _():
        if not first:
            for copy in loads():
                copy.wait()
        nb = layout.nb

        def add(idx, block):
            for at, chip, row, n in layout.pieces(idx // CORES):
                here = (idx % CORES, chip, slice(row, row + n))
                if first:
                    acc_ref[here] = block[at : at + n]
                else:
                    acc_ref[here] += block[at : at + n]

        if first:
            for idx in range(layout.used, CORES * layout.half):
                add(idx, jnp.zeros((TILE, TILE), jnp.float32))
        for j in range(0, nb, 2):
            part = dot_nt(rt_ref[0 : TILE * (j + 2), :], rt_ref[TILE * j : TILE * (j + 2), :])
            for i in range(j + 2):
                for jj in range(max(i, j), j + 2):
                    cut = slice(TILE * (jj - j), TILE * (jj - j + 1))
                    add(layout.number[i, jj], part[TILE * i : TILE * (i + 1), cut])
        stores = (
            pltpu.make_async_copy(acc_ref.at[me], mine_out, sem.at[0]),
            pltpu.make_async_copy(acc_ref.at[1 - me], other_out, sem.at[1]),
        )
        for copy in stores:
            copy.start()
        for copy in stores:
            copy.wait()


def gram_chunk(layout, core, arms, ft, angles, so_far):
    cols, samples = ft.shape
    run = (layout.plane, sum(layout.share), TILE)
    anywhere = pl.BlockSpec(memory_space=pl.ANY)
    if so_far is None:
        shape, place = jax.ShapeDtypeStruct(run, jnp.float32), anywhere
    else:
        shape, place = pltpu.VMEM(run, jnp.float32), pl.BlockSpec(memory_space=pltpu.VMEM)
    return pl.pallas_call(
        functools.partial(gram_kernel, layout, so_far is None),
        out_shape=(shape, shape),
        grid_spec=pltpu.PrefetchScalarGridSpec(
            num_scalar_prefetch=1,
            grid=(angles.shape[0],),
            in_specs=[
                pl.BlockSpec(arms.shape, lambda g, core: (0, 0)),
                pl.BlockSpec((cols, samples), lambda g, core: (0, 0))
                if so_far is None
                else pl.BlockSpec(memory_space=pltpu.VMEM),
                pl.BlockSpec(angles.shape, lambda g, core: (0, 0)),
            ]
            + ([] if so_far is None else [anywhere, anywhere]),
            out_specs=(place, place),
            scratch_shapes=[
                pltpu.VMEM((cols, samples), jnp.bfloat16),
                pltpu.VMEM((CORES, *run), jnp.float32),
                pltpu.SemaphoreType.DMA((2,)),
            ],
        ),
        compiler_params=pltpu.CompilerParams(vmem_limit_bytes=VMEM_BYTES if so_far is None else GRAM_BYTES),
        name="rotate_gram",
    )(core, arms, ft if so_far is None else pltpu.with_memory_space_constraint(ft, pltpu.VMEM), angles, *(() if so_far is None else so_far))


def split3(x):
    high = x.astype(jnp.bfloat16).astype(jnp.float32)
    rest = x - high
    middle = rest.astype(jnp.bfloat16).astype(jnp.float32)
    return high, middle, rest - middle


def outer_product(a, b):
    a1, a2, a3 = split3(a)
    b1, b2, b3 = split3(b)
    left = jnp.concatenate([a1, a1, a2, a2, a1, a3], axis=0).astype(jnp.bfloat16)
    right = jnp.concatenate([b1, b2, b1, b2, b3, b1], axis=0).astype(jnp.bfloat16)
    return lax.dot_general(
        left, right, (((0,), (0,)), ((), ())), preferred_element_type=jnp.float32
    )


def factor_block(a_ref, e_ref):
    lane = lax.broadcasted_iota(jnp.int32, (8, TILE), 1)
    sub = lax.broadcasted_iota(jnp.int32, (8, TILE), 0)
    strips = TILE // 8
    work = [a_ref[8 * t : 8 * t + 8, :] for t in range(strips)]

    def columns(x, r0):
        return [jnp.broadcast_to(x[:, r0 + j : r0 + j + 1], (8, TILE)) for j in range(8)]

    def row_of(x, j):
        return jnp.broadcast_to(x[j : j + 1, :], (8, TILE))

    top = columns(work[0], 0)
    for s in range(strips):
        r0 = 8 * s
        below = strips - 1 - s
        here = (lane >= r0) & (lane < r0 + 8)
        cur = jnp.where(here, jnp.where(lane == r0 + sub, 1.0, 0.0), work[s])
        if below:
            low = columns(work[s + 1], r0)
            top2 = columns(work[s], r0 + 8)
            low2 = columns(work[s + 1], r0 + 8)
            nxt = jnp.where(here, 0.0, work[s + 1])
        if below > 1:
            third = columns(work[s + 2], r0)
            nxt2 = jnp.where(here, 0.0, work[s + 2])
        for j in range(8):
            inv = 1.0 / row_of(top[j], j)
            m_top = jnp.where(sub > j, top[j] * inv, 0.0)
            m_low = low[j] * inv if below else None
            m_third = third[j] * inv if below > 1 else None
            for k in range(j + 1, 8):
                c = row_of(top[k], j)
                if k == j + 1:
                    top[k] = top[k] - jnp.where(sub > j, top[j] * c, 0.0) * inv
                else:
                    top[k] = top[k] - m_top * c
                if below:
                    low[k] = low[k] - m_low * c
                if below > 1:
                    third[k] = third[k] - m_third * c
            if below:
                for k in range(8):
                    c = row_of(top2[k], j)
                    if j < 7:
                        top2[k] = top2[k] - m_top * c
                    low2[k] = low2[k] - m_low * c
            row = row_of(cur, j)
            cur = cur - m_top * row
            if below:
                nxt = nxt - m_low * row
            if below > 1:
                nxt2 = nxt2 - m_third * row
        pivot = top[0]
        for j in range(1, 8):
            pivot = jnp.where(sub == j, top[j], pivot)
        scale = lax.rsqrt(pivot)
        cur = cur * scale
        later = jnp.where(lane >= r0 + 8, cur, 0.0)
        out = later
        for k in range(8):
            out = jnp.where((lane == r0 + k) & (sub <= k), top[k] * scale, out)
        a_ref[r0 : r0 + 8, :] = out
        e_ref[r0 : r0 + 8, :] = jnp.where(lane < r0 + 8, cur, 0.0)
        if below:
            work[s + 1] = nxt
            top = low2
        if below > 1:
            work[s + 2] = nxt2
        if below > 2:
            update = outer_product(later, cur)
            for t in range(s + 3, strips):
                work[t] = jnp.where(here, 0.0, work[t]) - update[8 * t : 8 * t + 8, :]


def dot_parts(a, b, contract):
    return lax.dot_general(
        a, b, (((contract,), (0,)), ((), ())), preferred_element_type=jnp.float32
    )


def product(left, right, contract):
    if left[0].shape[contract] <= TILE:
        pairs = ((0, 0), (0, 1), (1, 0), (1, 1), (0, 2), (2, 0))
        return dot_parts(
            jnp.concatenate([left[p] for p, _ in pairs], axis=contract),
            jnp.concatenate([right[q] for _, q in pairs], axis=0),
            contract,
        )
    m = left[0].shape[1 - contract]
    p = dot_parts(jnp.concatenate(left, axis=1 - contract), right[0], contract)
    q = dot_parts(jnp.concatenate(left[:2], axis=1 - contract), right[1], contract)
    r = dot_parts(left[0], right[2], contract)
    return p[:m] + ((p[m : 2 * m] + q[:m]) + ((p[2 * m :] + q[m:]) + r))


def parts3(x):
    return [v.astype(jnp.bfloat16) for v in split3(x)]


def cholesky_kernel(layout, scale, leading, core, *refs):
    n_in = 2 if leading else 6
    sources, refs = refs[:n_in], refs[n_in:]
    out_ref, refs = refs[0], refs[1:]
    if leading:
        inverse_ref, refs = refs[0], refs[1:]
    u_ref, g_ref, a_ref, e_ref, s_ref, p_ref, i_ref, in_sem, out_sem = refs
    me = core[0]
    nb, lead, early = layout.nb, layout.lead, layout.early
    begin, end = (0, lead) if leading else (lead, nb)
    edge = TILE * lead
    size = edge if leading else TILE * nb
    square = (slice(0, edge), slice(0, edge))
    corner = (slice(0, edge), slice(edge, TILE * nb))

    def part_loads(pair, lo, hi, to, sems):
        mine, other = pair
        n = hi - lo
        return [
            pltpu.make_async_copy(mine.at[lo:hi], g_ref.at[me, to : to + n], in_sem.at[sems]),
            pltpu.make_async_copy(
                other.at[lo:hi], g_ref.at[1 - me, to : to + n], in_sem.at[sems + 1]
            ),
        ]

    if leading:
        loads = part_loads(sources[:2], 0, early, 0, 0)
    else:
        first = layout.leading // CORES
        loads = part_loads(sources[2:4], 0, layout.half - early, early, 2)
        if first < early:
            loads += part_loads(sources[:2], first, early, first, 0)
        loads.append(pltpu.make_async_copy(sources[4].at[square], u_ref.at[square], in_sem.at[4]))
        loads.append(pltpu.make_async_copy(sources[5], i_ref, in_sem.at[5]))

    def store(k):
        here = (slice(TILE * k, TILE * (k + 1)), slice(0, size))
        return pltpu.make_async_copy(u_ref.at[here], out_ref.at[here], out_sem.at[k])

    def gram(i, j):
        n = layout.number[i, j]
        return g_ref[n % CORES, n // CORES] * scale

    def up(rows, cols):
        return [p_ref[q, rows, cols] for q in range(3)]

    def keep(rows, cols, value):
        for q, v in enumerate(parts3(value)):
            p_ref[q, rows, cols] = v

    for copy in loads:
        copy.start()
    for copy in loads:
        copy.wait()

    stores = []
    if not leading:
        right = slice(edge, size)
        for k in range(lead):
            rows, cols = slice(TILE * k, TILE * (k + 1)), slice(TILE * k, edge)
            keep(rows, cols, u_ref[rows, cols])
        for k in range(lead):
            rows = slice(TILE * k, TILE * (k + 1))
            above = slice(0, TILE * k)
            value = jnp.concatenate([gram(k, j) for j in range(lead, nb)], axis=1)
            if k:
                value = value - product(up(above, rows), up(above, right), 0)
            value = product(parts3(i_ref[k]), parts3(value), 1)
            u_ref[rows, right] = value
            keep(rows, right, value)
        stores.append(
            pltpu.make_async_copy(u_ref.at[corner], out_ref.at[corner], out_sem.at[0])
        )
        stores[0].start()

    def body(i, carry):
        for k in range(begin, end):
            h = k % 2
            r0 = TILE * (k - h)
            c0 = TILE * k

            @pl.when(i == k)
            def _(k=k, h=h, r0=r0, c0=c0):
                if h == 0:
                    for hh in range(2):
                        for j in range(k, size // TILE):
                            if j < k + hh:
                                block = jnp.zeros((TILE, TILE), jnp.float32)
                            else:
                                block = gram(k + hh, j)
                            s_ref[TILE * hh : TILE * (hh + 1), TILE * j : TILE * (j + 1)] = block
                    if r0:
                        panel = slice(r0, r0 + 2 * TILE)
                        s_ref[:, r0:size] -= product(
                            up(slice(0, r0), panel), up(slice(0, r0), slice(r0, size)), 0
                        )
                else:
                    above = slice(r0, c0)
                    s_ref[TILE:, c0:size] -= product(
                        up(above, slice(c0, c0 + TILE)), up(above, slice(c0, size)), 0
                    )
                a_ref[...] = s_ref[TILE * h : TILE * (h + 1), c0 : c0 + TILE]

        factor_block(a_ref, e_ref)
        for k in range(begin, end):
            h = k % 2
            c0 = TILE * k

            @pl.when(i == k)
            def _(k=k, h=h, c0=c0):
                rows = slice(c0, c0 + TILE)
                if c0:
                    u_ref[rows, 0:c0] = jnp.zeros((TILE, c0), jnp.float32)
                u_ref[rows, c0 : c0 + TILE] = a_ref[...]
                if leading:
                    i_ref[k] = e_ref[...]
                if c0 + TILE < size:
                    rest = slice(c0 + TILE, size)
                    solved = product(
                        parts3(e_ref[...]), parts3(s_ref[TILE * h : TILE * (h + 1), rest]), 1
                    )
                    u_ref[rows, rest] = solved
                    keep(rows, rest, solved)
                store(k).start()

        return carry

    lax.fori_loop(begin, end, body, 0)
    if leading:
        stores.append(pltpu.make_async_copy(i_ref, inverse_ref, in_sem.at[4]))
        stores[0].start()
    stores += [store(k) for k in range(begin, end)]
    for copy in stores:
        copy.wait()


def cholesky_part(layout, core, groups, so_far, scale):
    size = layout.nb * TILE
    leading = so_far is None
    anywhere = pl.BlockSpec(memory_space=pl.ANY)
    sources = [pltpu.with_memory_space_constraint(x, pltpu.VMEM) for pair in groups for x in pair]
    n_blocks = len(sources)
    sources += [] if leading else list(so_far)
    factor = jax.ShapeDtypeStruct((size, size), jnp.float32)
    inverses = jax.ShapeDtypeStruct((layout.lead, TILE, TILE), jnp.float32)
    blocks = layout.lead if leading else layout.nb - layout.lead
    return pl.pallas_call(
        functools.partial(cholesky_kernel, layout, scale, leading),
        out_shape=(factor, inverses) if leading else factor,
        grid_spec=pltpu.PrefetchScalarGridSpec(
            num_scalar_prefetch=1,
            grid=(1,),
            in_specs=[pl.BlockSpec(memory_space=pltpu.VMEM)] * n_blocks
            + [anywhere] * (len(sources) - n_blocks),
            out_specs=(anywhere, anywhere) if leading else anywhere,
            scratch_shapes=[
                pltpu.VMEM((size, size), jnp.float32),
                pltpu.VMEM((CORES, layout.half, TILE, TILE), jnp.float32),
                pltpu.VMEM((TILE, TILE), jnp.float32),
                pltpu.VMEM((TILE, TILE), jnp.float32),
                pltpu.VMEM((2 * TILE, size), jnp.float32),
                pltpu.VMEM((3, size, size), jnp.bfloat16),
                pltpu.VMEM((layout.lead, TILE, TILE), jnp.float32),
                pltpu.SemaphoreType.DMA((6,)),
                pltpu.SemaphoreType.DMA((layout.nb,)),
            ],
        ),
        input_output_aliases={} if leading else {len(sources) - 1: 0},
        cost_estimate=pl.CostEstimate(
            flops=40 * blocks * size**2 * TILE, transcendentals=0, bytes_accessed=12 * size**2
        ),
        compiler_params=pltpu.CompilerParams(vmem_limit_bytes=VMEM_BYTES),
        name="cholesky",
    )(core, *sources)


def swap_cores(x):
    return lax.ppermute(x, "core", [(0, 1), (1, 0)])


def gather_plane(copies):
    return lax.all_to_all(copies, PLANE_AXES, split_axis=0, concat_axis=0, tiled=True)


def shards(records, offsets, column_map, angles):
    parts = lax.axis_size(GAUGE_AXES)
    rows, cols_here = records.shape
    cols = column_map.shape[0]
    core = lax.axis_index("core").astype(jnp.int32).reshape(1)
    records_t = records.T
    arms = column_map.reshape(-1, TILE)
    angles = angles.reshape(-1, TILE)
    layout = Layout(cols // TILE, lax.axis_size(PLANE_AXES))
    acc = None
    for filtered in filter_records(records_t, offsets, parts):
        regrouped = lax.all_to_all(filtered, GAUGE_AXES, split_axis=0, concat_axis=0, tiled=True)
        acc = gram_chunk(layout, core, arms, regrouped.reshape(cols, -1), angles, acc)
    mine, other = acc
    mine = mine + swap_cores(other)
    spread = lax.all_to_all(mine, PLANE_AXES, split_axis=0, concat_axis=0, tiled=True).sum(0)
    scale = 1.0 / (rows * lax.axis_size(SAMPLE_AXES))
    early, late = (
        jnp.broadcast_to(x[None], (layout.plane, *x.shape))
        for x in jnp.split(spread, [layout.share[0]])
    )
    early = gather_plane(early)
    late, early = lax.optimization_barrier((late, early))
    late = gather_plane(late)
    early, late = (g.reshape(-1, TILE, TILE) for g in (early, late))
    groups = [(early, swap_cores(early))]
    upper, inverses = cholesky_part(layout, core, groups, None, scale)
    late, upper = lax.optimization_barrier((late, upper))
    groups.append((late, swap_cores(late)))
    return cholesky_part(layout, core, groups, (upper, inverses), scale)


def solution(mesh):
    devices = mesh.devices
    tm, gauge = devices.shape
    side = int(round(tm**0.5))
    fine = Mesh(
        devices.reshape(side, tm // side, gauge // CORES, CORES), SAMPLE_AXES + GAUGE_AXES
    )
    placed = (P(SAMPLE_AXES, GAUGE_AXES), P(SAMPLE_AXES), P(), P())
    return jax.shard_map(shards, mesh=fine, in_specs=placed, out_specs=P(), check_vma=False)
```

```python
import functools

import jax
import jax.numpy as jnp
from jax import lax
from jax.experimental import pallas as pl
from jax.experimental.pallas import tpu as pltpu
from jax.sharding import Mesh
from jax.sharding import PartitionSpec as P

BLOCK = 1024
BAND = 64
TILE = 128
CORES = 2
SAMPLE_AXES = ("z", "x")
GAUGE_AXES = ("y", "core")
PLANE_AXES = ("z", "x", "y")
HIGHEST = lax.Precision.HIGHEST
VMEM_BYTES = 54 * 1024 * 1024
GRAM_BYTES = 50 * 1024 * 1024
FILTER_BYTES = 54 * 1024 * 1024
STEPS = 4


class Layout:
    def __init__(self, nb, plane):
        self.nb, self.plane = nb, plane
        self.lead = lead = nb // 4 * 2
        order = [(i, j) for i in range(lead) for j in range(i, lead)]
        self.leading = len(order)
        order += [(i, j) for i in range(nb) for j in range(max(i, lead), nb)]
        self.number = {ij: n for n, ij in enumerate(order)}
        self.used = len(order)
        step = max(1, 8 * plane // TILE)
        self.early = -(-(-(-self.leading // CORES)) // step) * step
        self.half = -(-(-(-self.used // CORES)) // step) * step
        self.share = (self.early * TILE // plane, (self.half - self.early) * TILE // plane)

    def pieces(self, position):
        late = position >= self.early
        share = self.share[late]
        base = self.share[0] if late else 0
        row = (position - (self.early if late else 0)) * TILE
        at, out = 0, []
        while at < TILE:
            chip, inside = divmod(row + at, share)
            n = min(share - inside, TILE - at)
            out.append((at, chip, base + inside, n))
            at += n
        return out


def dot_nt(a, b):
    return lax.dot_general(a, b, (((1,), (1,)), ((), ())), preferred_element_type=jnp.float32)


def filter_kernel(offsets, x_ref, head_ref, tail_ref):
    parts, split = tail_ref.shape[0], head_ref.shape[2]
    step = pl.program_id(0)
    blocks = x_ref.shape[1] // BLOCK // parts
    for b in range(parts * blocks):
        start = offsets[step * parts * blocks + b]
        x = x_ref[:, b * BLOCK : (b + 1) * BLOCK]
        sample = lax.broadcasted_iota(jnp.int32, (1, BLOCK), 1)
        inside = jnp.where((sample >= start) & (sample < start + BAND), 1.0, 0.0)
        mask = jnp.broadcast_to(inside.astype(jnp.bfloat16), (TILE, BLOCK))
        baseline = dot_nt(x, mask) * (1.0 / BAND)
        for t in range(0, BLOCK, TILE):
            value = (x[:, t : t + TILE].astype(jnp.float32) - baseline).astype(jnp.bfloat16)
            here = b % blocks * BLOCK + t
            if here < split:
                head_ref[step * parts + b // blocks, :, here : here + TILE] = value
            else:
                tail_ref[b // blocks, :, here - split : here - split + TILE] = value


def filter_records(records_t, offsets, parts):
    rows, samples = records_t.shape
    each = samples // parts
    tail = BLOCK // 2
    return pl.pallas_call(
        filter_kernel,
        out_shape=(
            pltpu.VMEM((parts, rows, each - tail), jnp.bfloat16),
            jax.ShapeDtypeStruct((parts, rows, tail), jnp.bfloat16),
        ),
        grid_spec=pltpu.PrefetchScalarGridSpec(
            num_scalar_prefetch=1,
            grid=(STEPS,),
            in_specs=[pl.BlockSpec((rows, samples // STEPS), lambda d, off: (0, d))],
            out_specs=(
                pl.BlockSpec(memory_space=pltpu.VMEM),
                pl.BlockSpec((parts // STEPS, rows, tail), lambda d, off: (d, 0, 0)),
            ),
        ),
        compiler_params=pltpu.CompilerParams(vmem_limit_bytes=FILTER_BYTES),
        name="drift_filter",
    )(offsets, records_t)


def gram_kernel(layout, first, core, *refs):
    if first:
        map_ref, ft_ref, angle_ref, mine_out, other_out, rt_ref, acc_ref, sem = refs
        mine_in = other_in = None
    else:
        map_ref, ft_ref, angle_ref, mine_in, other_in, mine_out, other_out, rt_ref, acc_ref, sem = refs
    step = pl.program_id(0)
    me = core[0]

    def loads():
        return (
            pltpu.make_async_copy(mine_in, acc_ref.at[me], sem.at[0]),
            pltpu.make_async_copy(other_in, acc_ref.at[1 - me], sem.at[1]),
        )

    if not first:

        @pl.when(step == 0)
        def _():
            for copy in loads():
                copy.start()

    ft = ft_ref[...]
    cols, samples = ft.shape
    lanes = map_ref.shape[1]
    steps = pl.num_programs(0)

    def down(row):
        return jnp.broadcast_to(row, (lanes, lanes)).T

    def arm(k):
        source = down(map_ref[pl.ds(k * steps + step, 1), :].astype(jnp.float32))
        index = lax.broadcasted_iota(jnp.int32, (lanes, lanes), 1).astype(jnp.float32)
        pick = [jnp.where(source - c == index, 1.0, 0.0) for c in range(0, cols, lanes)]
        pick = jnp.concatenate(pick, axis=1).astype(jnp.bfloat16)
        return jnp.dot(pick, ft, preferred_element_type=jnp.float32)

    first_arm, middle_arm, last_arm = (arm(k) for k in range(3))
    shear = 2.0 * middle_arm - first_arm - last_arm
    angle = angle_ref[pl.ds(step, 1), :]
    cosine, sine = jnp.cos(angle), jnp.sin(angle)
    cos_sq, sin_sq, mixed = (
        jnp.tile(down(c), (1, samples // lanes))
        for c in (cosine * cosine, sine * sine, sine * cosine)
    )
    twist = shear * mixed
    along_x = first_arm * cos_sq + last_arm * sin_sq + twist
    along_y = first_arm * sin_sq + last_arm * cos_sq - twist
    shear_new = 2.0 * (last_arm - first_arm) * mixed + shear * (cos_sq - sin_sq)
    per_arm = rt_ref.shape[0] // 3
    here = pl.multiple_of(step * lanes, lanes)
    for k, value in enumerate((along_x, along_y, shear_new)):
        rt_ref[pl.ds(k * per_arm + here, lanes), :] = value.astype(jnp.bfloat16)

    @pl.when(step == pl.num_programs(0) - 1)
    def _():
        if not first:
            for copy in loads():
                copy.wait()
        nb = layout.nb

        def add(idx, block):
            for at, chip, row, n in layout.pieces(idx // CORES):
                here = (idx % CORES, chip, slice(row, row + n))
                if first:
                    acc_ref[here] = block[at : at + n]
                else:
                    acc_ref[here] += block[at : at + n]

        if first:
            for idx in range(layout.used, CORES * layout.half):
                add(idx, jnp.zeros((TILE, TILE), jnp.float32))
        for j in range(0, nb, 2):
            part = dot_nt(rt_ref[0 : TILE * (j + 2), :], rt_ref[TILE * j : TILE * (j + 2), :])
            for i in range(j + 2):
                for jj in range(max(i, j), j + 2):
                    cut = slice(TILE * (jj - j), TILE * (jj - j + 1))
                    add(layout.number[i, jj], part[TILE * i : TILE * (i + 1), cut])
        stores = (
            pltpu.make_async_copy(acc_ref.at[me], mine_out, sem.at[0]),
            pltpu.make_async_copy(acc_ref.at[1 - me], other_out, sem.at[1]),
        )
        for copy in stores:
            copy.start()
        for copy in stores:
            copy.wait()


def gram_chunk(layout, core, arms, ft, angles, so_far):
    cols, samples = ft.shape
    run = (layout.plane, sum(layout.share), TILE)
    anywhere = pl.BlockSpec(memory_space=pl.ANY)
    if so_far is None:
        shape, place = jax.ShapeDtypeStruct(run, jnp.float32), anywhere
    else:
        shape, place = pltpu.VMEM(run, jnp.float32), pl.BlockSpec(memory_space=pltpu.VMEM)
    return pl.pallas_call(
        functools.partial(gram_kernel, layout, so_far is None),
        out_shape=(shape, shape),
        grid_spec=pltpu.PrefetchScalarGridSpec(
            num_scalar_prefetch=1,
            grid=(angles.shape[0],),
            in_specs=[
                pl.BlockSpec(arms.shape, lambda g, core: (0, 0)),
                pl.BlockSpec((cols, samples), lambda g, core: (0, 0))
                if so_far is None
                else pl.BlockSpec(memory_space=pltpu.VMEM),
                pl.BlockSpec(angles.shape, lambda g, core: (0, 0)),
            ]
            + ([] if so_far is None else [anywhere, anywhere]),
            out_specs=(place, place),
            scratch_shapes=[
                pltpu.VMEM((cols, samples), jnp.bfloat16),
                pltpu.VMEM((CORES, *run), jnp.float32),
                pltpu.SemaphoreType.DMA((2,)),
            ],
        ),
        compiler_params=pltpu.CompilerParams(vmem_limit_bytes=VMEM_BYTES if so_far is None else GRAM_BYTES),
        name="rotate_gram",
    )(core, arms, ft if so_far is None else pltpu.with_memory_space_constraint(ft, pltpu.VMEM), angles, *(() if so_far is None else so_far))


def split3(x):
    high = x.astype(jnp.bfloat16).astype(jnp.float32)
    rest = x - high
    middle = rest.astype(jnp.bfloat16).astype(jnp.float32)
    return high, middle, rest - middle


def outer_product(a, b):
    a1, a2, a3 = split3(a)
    b1, b2, b3 = split3(b)
    left = jnp.concatenate([a1, a1, a2, a2, a1, a3], axis=0).astype(jnp.bfloat16)
    right = jnp.concatenate([b1, b2, b1, b2, b3, b1], axis=0).astype(jnp.bfloat16)
    return lax.dot_general(
        left, right, (((0,), (0,)), ((), ())), preferred_element_type=jnp.float32
    )


def factor_block(a_ref, e_ref):
    lane = lax.broadcasted_iota(jnp.int32, (8, TILE), 1)
    sub = lax.broadcasted_iota(jnp.int32, (8, TILE), 0)
    strips = TILE // 8
    work = [a_ref[8 * t : 8 * t + 8, :] for t in range(strips)]

    def columns(x, r0):
        return [jnp.broadcast_to(x[:, r0 + j : r0 + j + 1], (8, TILE)) for j in range(8)]

    def row_of(x, j):
        return jnp.broadcast_to(x[j : j + 1, :], (8, TILE))

    top = columns(work[0], 0)
    for s in range(strips):
        r0 = 8 * s
        below = strips - 1 - s
        here = (lane >= r0) & (lane < r0 + 8)
        cur = jnp.where(here, jnp.where(lane == r0 + sub, 1.0, 0.0), work[s])
        if below:
            low = columns(work[s + 1], r0)
            top2 = columns(work[s], r0 + 8)
            low2 = columns(work[s + 1], r0 + 8)
            nxt = jnp.where(here, 0.0, work[s + 1])
        if below > 1:
            third = columns(work[s + 2], r0)
            nxt2 = jnp.where(here, 0.0, work[s + 2])
        for j in range(8):
            inv = 1.0 / row_of(top[j], j)
            m_top = jnp.where(sub > j, top[j] * inv, 0.0)
            m_low = low[j] * inv if below else None
            m_third = third[j] * inv if below > 1 else None
            for k in range(j + 1, 8):
                c = row_of(top[k], j)
                if k == j + 1:
                    top[k] = top[k] - jnp.where(sub > j, top[j] * c, 0.0) * inv
                else:
                    top[k] = top[k] - m_top * c
                if below:
                    low[k] = low[k] - m_low * c
                if below > 1:
                    third[k] = third[k] - m_third * c
            if below:
                for k in range(8):
                    c = row_of(top2[k], j)
                    if j < 7:
                        top2[k] = top2[k] - m_top * c
                    low2[k] = low2[k] - m_low * c
            row = row_of(cur, j)
            cur = cur - m_top * row
            if below:
                nxt = nxt - m_low * row
            if below > 1:
                nxt2 = nxt2 - m_third * row
        pivot = top[0]
        for j in range(1, 8):
            pivot = jnp.where(sub == j, top[j], pivot)
        scale = lax.rsqrt(pivot)
        cur = cur * scale
        later = jnp.where(lane >= r0 + 8, cur, 0.0)
        out = later
        for k in range(8):
            out = jnp.where((lane == r0 + k) & (sub <= k), top[k] * scale, out)
        a_ref[r0 : r0 + 8, :] = out
        e_ref[r0 : r0 + 8, :] = jnp.where(lane < r0 + 8, cur, 0.0)
        if below:
            work[s + 1] = nxt
            top = low2
        if below > 1:
            work[s + 2] = nxt2
        if below > 2:
            update = outer_product(later, cur)
            for t in range(s + 3, strips):
                work[t] = jnp.where(here, 0.0, work[t]) - update[8 * t : 8 * t + 8, :]


def dot_parts(a, b, contract):
    return lax.dot_general(
        a, b, (((contract,), (0,)), ((), ())), preferred_element_type=jnp.float32
    )


def product(left, right, contract):
    if left[0].shape[contract] <= TILE:
        pairs = ((0, 0), (0, 1), (1, 0), (1, 1), (0, 2), (2, 0))
        return dot_parts(
            jnp.concatenate([left[p] for p, _ in pairs], axis=contract),
            jnp.concatenate([right[q] for _, q in pairs], axis=0),
            contract,
        )
    m = left[0].shape[1 - contract]
    p = dot_parts(jnp.concatenate(left, axis=1 - contract), right[0], contract)
    q = dot_parts(jnp.concatenate(left[:2], axis=1 - contract), right[1], contract)
    r = dot_parts(left[0], right[2], contract)
    return p[:m] + ((p[m : 2 * m] + q[:m]) + ((p[2 * m :] + q[m:]) + r))


def parts3(x):
    return [v.astype(jnp.bfloat16) for v in split3(x)]


def cholesky_kernel(layout, scale, leading, core, *refs):
    n_in = 2 if leading else 6
    sources, refs = refs[:n_in], refs[n_in:]
    out_ref, refs = refs[0], refs[1:]
    if leading:
        inverse_ref, refs = refs[0], refs[1:]
    u_ref, g_ref, a_ref, e_ref, s_ref, p_ref, i_ref, in_sem, out_sem = refs
    me = core[0]
    nb, lead, early = layout.nb, layout.lead, layout.early
    begin, end = (0, lead) if leading else (lead, nb)
    edge = TILE * lead
    size = edge if leading else TILE * nb
    square = (slice(0, edge), slice(0, edge))
    corner = (slice(0, edge), slice(edge, TILE * nb))

    def part_loads(pair, lo, hi, to, sems):
        mine, other = pair
        n = hi - lo
        return [
            pltpu.make_async_copy(mine.at[lo:hi], g_ref.at[me, to : to + n], in_sem.at[sems]),
            pltpu.make_async_copy(
                other.at[lo:hi], g_ref.at[1 - me, to : to + n], in_sem.at[sems + 1]
            ),
        ]

    if leading:
        loads = part_loads(sources[:2], 0, early, 0, 0)
    else:
        first = layout.leading // CORES
        loads = part_loads(sources[2:4], 0, layout.half - early, early, 2)
        if first < early:
            loads += part_loads(sources[:2], first, early, first, 0)
        loads.append(pltpu.make_async_copy(sources[4].at[square], u_ref.at[square], in_sem.at[4]))
        loads.append(pltpu.make_async_copy(sources[5], i_ref, in_sem.at[5]))

    def store(k):
        here = (slice(TILE * k, TILE * (k + 1)), slice(0, size))
        return pltpu.make_async_copy(u_ref.at[here], out_ref.at[here], out_sem.at[k])

    def gram(i, j):
        n = layout.number[i, j]
        return g_ref[n % CORES, n // CORES] * scale

    def up(rows, cols):
        return [p_ref[q, rows, cols] for q in range(3)]

    def keep(rows, cols, value):
        for q, v in enumerate(parts3(value)):
            p_ref[q, rows, cols] = v

    for copy in loads:
        copy.start()
    for copy in loads:
        copy.wait()

    stores = []
    if not leading:
        right = slice(edge, size)
        for k in range(lead):
            rows, cols = slice(TILE * k, TILE * (k + 1)), slice(TILE * k, edge)
            keep(rows, cols, u_ref[rows, cols])
        for k in range(lead):
            rows = slice(TILE * k, TILE * (k + 1))
            above = slice(0, TILE * k)
            value = jnp.concatenate([gram(k, j) for j in range(lead, nb)], axis=1)
            if k:
                value = value - product(up(above, rows), up(above, right), 0)
            value = product(parts3(i_ref[k]), parts3(value), 1)
            u_ref[rows, right] = value
            keep(rows, right, value)
        stores.append(
            pltpu.make_async_copy(u_ref.at[corner], out_ref.at[corner], out_sem.at[0])
        )
        stores[0].start()

    def body(i, carry):
        for k in range(begin, end):
            h = k % 2
            r0 = TILE * (k - h)
            c0 = TILE * k

            @pl.when(i == k)
            def _(k=k, h=h, r0=r0, c0=c0):
                if h == 0:
                    for hh in range(2):
                        for j in range(k, size // TILE):
                            if j < k + hh:
                                block = jnp.zeros((TILE, TILE), jnp.float32)
                            else:
                                block = gram(k + hh, j)
                            s_ref[TILE * hh : TILE * (hh + 1), TILE * j : TILE * (j + 1)] = block
                    if r0:
                        panel = slice(r0, r0 + 2 * TILE)
                        s_ref[:, r0:size] -= product(
                            up(slice(0, r0), panel), up(slice(0, r0), slice(r0, size)), 0
                        )
                else:
                    above = slice(r0, c0)
                    s_ref[TILE:, c0:size] -= product(
                        up(above, slice(c0, c0 + TILE)), up(above, slice(c0, size)), 0
                    )
                a_ref[...] = s_ref[TILE * h : TILE * (h + 1), c0 : c0 + TILE]

        factor_block(a_ref, e_ref)
        for k in range(begin, end):
            h = k % 2
            c0 = TILE * k

            @pl.when(i == k)
            def _(k=k, h=h, c0=c0):
                rows = slice(c0, c0 + TILE)
                if c0:
                    u_ref[rows, 0:c0] = jnp.zeros((TILE, c0), jnp.float32)
                u_ref[rows, c0 : c0 + TILE] = a_ref[...]
                if leading:
                    i_ref[k] = e_ref[...]
                if c0 + TILE < size:
                    rest = slice(c0 + TILE, size)
                    solved = product(
                        parts3(e_ref[...]), parts3(s_ref[TILE * h : TILE * (h + 1), rest]), 1
                    )
                    u_ref[rows, rest] = solved
                    keep(rows, rest, solved)
                store(k).start()

        return carry

    lax.fori_loop(begin, end, body, 0)
    if leading:
        stores.append(pltpu.make_async_copy(i_ref, inverse_ref, in_sem.at[4]))
        stores[0].start()
    stores += [store(k) for k in range(begin, end)]
    for copy in stores:
        copy.wait()


def cholesky_part(layout, core, groups, so_far, scale):
    size = layout.nb * TILE
    leading = so_far is None
    anywhere = pl.BlockSpec(memory_space=pl.ANY)
    sources = [pltpu.with_memory_space_constraint(x, pltpu.VMEM) for pair in groups for x in pair]
    n_blocks = len(sources)
    sources += [] if leading else list(so_far)
    factor = jax.ShapeDtypeStruct((size, size), jnp.float32)
    inverses = jax.ShapeDtypeStruct((layout.lead, TILE, TILE), jnp.float32)
    blocks = layout.lead if leading else layout.nb - layout.lead
    return pl.pallas_call(
        functools.partial(cholesky_kernel, layout, scale, leading),
        out_shape=(factor, inverses) if leading else factor,
        grid_spec=pltpu.PrefetchScalarGridSpec(
            num_scalar_prefetch=1,
            grid=(1,),
            in_specs=[pl.BlockSpec(memory_space=pltpu.VMEM)] * n_blocks
            + [anywhere] * (len(sources) - n_blocks),
            out_specs=(anywhere, anywhere) if leading else anywhere,
            scratch_shapes=[
                pltpu.VMEM((size, size), jnp.float32),
                pltpu.VMEM((CORES, layout.half, TILE, TILE), jnp.float32),
                pltpu.VMEM((TILE, TILE), jnp.float32),
                pltpu.VMEM((TILE, TILE), jnp.float32),
                pltpu.VMEM((2 * TILE, size), jnp.float32),
                pltpu.VMEM((3, size, size), jnp.bfloat16),
                pltpu.VMEM((layout.lead, TILE, TILE), jnp.float32),
                pltpu.SemaphoreType.DMA((6,)),
                pltpu.SemaphoreType.DMA((layout.nb,)),
            ],
        ),
        input_output_aliases={} if leading else {len(sources) - 1: 0},
        cost_estimate=pl.CostEstimate(
            flops=40 * blocks * size**2 * TILE, transcendentals=0, bytes_accessed=12 * size**2
        ),
        compiler_params=pltpu.CompilerParams(vmem_limit_bytes=VMEM_BYTES),
        name="cholesky",
    )(core, *sources)


def swap_cores(x):
    return lax.ppermute(x, "core", [(0, 1), (1, 0)])


def sum_kernel(x_ref, early_ref, late_ref):
    total = x_ref[0]
    for chip in range(1, x_ref.shape[0]):
        total = total + x_ref[chip]
    split = early_ref.shape[1]
    for chip in range(x_ref.shape[0]):
        early_ref[chip] = total[:split]
        late_ref[chip] = total[split:]


def sum_and_copy(layout, spread):
    here = pl.BlockSpec(memory_space=pltpu.VMEM)
    return pl.pallas_call(
        sum_kernel,
        out_shape=(
            pltpu.VMEM((layout.plane, layout.share[0], TILE), jnp.float32),
            jax.ShapeDtypeStruct((layout.plane, layout.share[1], TILE), jnp.float32),
        ),
        grid=(1,),
        in_specs=[here],
        out_specs=(
            here,
            pl.BlockSpec((layout.plane, layout.share[1], TILE), lambda g: (0, 0, 0)),
        ),
        compiler_params=pltpu.CompilerParams(vmem_limit_bytes=GRAM_BYTES),
        name="sum_and_copy",
    )(pltpu.with_memory_space_constraint(spread, pltpu.VMEM))


def gather_plane(copies):
    return lax.all_to_all(copies, PLANE_AXES, split_axis=0, concat_axis=0, tiled=True)


def shards(records, offsets, column_map, angles):
    parts = lax.axis_size(GAUGE_AXES)
    rows, cols_here = records.shape
    cols = column_map.shape[0]
    core = lax.axis_index("core").astype(jnp.int32).reshape(1)
    records_t = records.T
    arms = column_map.reshape(-1, TILE)
    angles = angles.reshape(-1, TILE)
    layout = Layout(cols // TILE, lax.axis_size(PLANE_AXES))
    acc = None
    for filtered in filter_records(records_t, offsets, parts):
        regrouped = lax.all_to_all(filtered, GAUGE_AXES, split_axis=0, concat_axis=0, tiled=True)
        acc = gram_chunk(layout, core, arms, regrouped.reshape(cols, -1), angles, acc)
    mine, other = acc
    mine = mine + swap_cores(other)
    spread = lax.all_to_all(mine, PLANE_AXES, split_axis=0, concat_axis=0, tiled=True)
    scale = 1.0 / (rows * lax.axis_size(SAMPLE_AXES))
    early, late = sum_and_copy(layout, spread)
    early = gather_plane(early)
    late, early = lax.optimization_barrier((late, early))
    late = gather_plane(late)
    early, late = (g.reshape(-1, TILE, TILE) for g in (early, late))
    groups = [(early, swap_cores(early))]
    upper, inverses = cholesky_part(layout, core, groups, None, scale)
    late, upper = lax.optimization_barrier((late, upper))
    groups.append((late, swap_cores(late)))
    return cholesky_part(layout, core, groups, (upper, inverses), scale)


def solution(mesh):
    devices = mesh.devices
    tm, gauge = devices.shape
    side = int(round(tm**0.5))
    fine = Mesh(
        devices.reshape(side, tm // side, gauge // CORES, CORES), SAMPLE_AXES + GAUGE_AXES
    )
    placed = (P(SAMPLE_AXES, GAUGE_AXES), P(SAMPLE_AXES), P(), P())
    return jax.shard_map(shards, mesh=fine, in_specs=placed, out_specs=P(), check_vma=False)
```
